32 devices in a mesh: sub: 16 (over z, y, x), mode: 2 (over core).
Axes of the slice: x: 2, y: 2, z: 4, core: 2. Of those that a mesh axis runs over, the one named last changes fastest.
Arguments:
- coupling: bfloat16 [1024, 64, 128], P('sub'), may hold values from -0.5 to 0.5
- coupling_pairs: int32 [1024, 2], P('sub'), may hold values from 0 to 3, as said below
- modes: bfloat16 [1024, 256, 256], P('sub', None, 'mode'), may hold values from -6 to 6
- mode_weights: bfloat16 [1024, 256], P('sub', 'mode'), may hold values from 0 to 1, as said below
- parent_of: int32 [1024, 1], P('sub'), may hold values from 0 to 15; in each aligned block of 64 rows (0 to 63, 64 to 127, ...) at most 8 rows name the same one
- row_block: int32 [1024], P('sub'), may hold values from 0 to 7
- parent_modes: bfloat16 [16, 512, 256], P('sub'), may hold values from -1 to 1
- parent_eigs: float32 [16, 256], P('sub'), may hold values from 0.02 to 0.5
Outputs:
- strengths: float32 [1024, 256], P('sub', 'mode')
The draws below stay inside these ranges and needn't reach their ends.
Inputs may be any that keep to these rules, and one draw needn't show every extreme that they name: `coupling_pairs`: within each child the 2 block indices are distinct. `parent_of`: the 64 children of one index of sub name any one parent at most 8 times; some parent is named exactly 8 times by some index's children. `mode_weights`: Positive.
All inputs are finite; a program needn't handle non-finite values.
Results may differ from the reference program's by a relative error of at most 0.0015.
Values may be sent and summed in bfloat16 or wider, within the bound.
A program may use at most 128 MiB of HBM per device.

```python
import math
import jax
import jax.numpy as jnp
import numpy as np
from jax import lax

M = 256
MP = 256
BLK = 64
NBC = 4
KB = 2
SB = 8
CH_DEV = 64
CHILDREN = 1024
PARENTS = 16
CAPD = 8
N_SUB = 16


def draw_coupling_pairs(key, part):
    scores = jax.random.randint(jax.random.fold_in(key, 11), (CHILDREN, NBC), 0, 1 << 20)
    scores = scores * NBC + jnp.arange(NBC, dtype=jnp.int32)[None, :]
    order = jnp.argsort(scores, axis=1, stable=True)
    return order[:, :KB].astype(jnp.int32)


def draw_mode_weights(key, part):
    level = jax.random.uniform(jax.random.fold_in(key, 23), (CHILDREN, M), jnp.float32, math.log(0.5), 0.0)
    falloff = jnp.arange(M, dtype=jnp.float32) / (M - 1)
    values = jnp.exp(level) * jnp.exp(-math.log(3.0) * falloff)[None, :]
    return values.astype(jnp.bfloat16)


def draw_parent_modes(key, part):
    base = jax.random.normal(jax.random.fold_in(key, 31), (PARENTS, SB * BLK, MP), jnp.float32)
    left = jax.random.normal(jax.random.fold_in(key, 37), (PARENTS, SB * BLK, 1), jnp.float32)
    right = jax.random.normal(jax.random.fold_in(key, 41), (PARENTS, 1, MP), jnp.float32)
    base = jnp.clip(base, -4.0, 4.0)
    left = jnp.clip(left, -3.0, 3.0)
    right = jnp.clip(right, -3.0, 3.0)
    return ((base + 0.6 * left * right) / 10.0).astype(jnp.bfloat16)


def place_ends(result, own_key, least, largest):
    spot = [jax.random.randint(jax.random.fold_in(own_key, axis), (), 0, length) for axis, length in enumerate(result.shape)]
    widest = result.shape.index(max(result.shape))
    beside = spot[:widest] + [(spot[widest] + 1) % result.shape[widest]] + spot[widest + 1:]
    return result.at[tuple(spot)].set(least).at[tuple(beside)].set(largest)


def block_levels(rng, extent, shards, least, top_value):
    factor_of = 1.0
    for dim, shards_of in shards:
        draws = jax.random.uniform(jax.random.fold_in(jax.random.fold_in(rng, 6), dim), (shards_of,), jnp.float32, least / len(shards), top_value / len(shards))
        factor_of = factor_of * jnp.repeat(jnp.exp(draws), extent[dim] // shards_of).reshape((-1,) + (1,) * (len(extent) - 1 - dim))
    return factor_of


def deal_out(rng, own, number, rows, count, top, bound, skew):
    order = jax.random.permutation(rng, count)
    heavy_load, ordinary = portions_of(count, rows * top, bound, skew, True), portions_of(count, rows * top, bound, skew, False)
    places = jnp.arange(count)

    def named(lengths, rotation):
        used = int((lengths > 0).sum())
        fixed = max(1, used // 4)
        passed = fixed + (places - fixed + rotation * (used - fixed)) % max(1, count - fixed)
        return jnp.zeros((count,), jnp.int32).at[order[jnp.where(places < fixed, places, passed)]].set(jnp.asarray(lengths, jnp.int32))

    lengths = jnp.where(number % 4 == 0, named(heavy_load, number // 4), named(ordinary, number - number // 4 - 1))
    mixed = jax.random.permutation(jax.random.fold_in(own, 3), count)
    donor, taker = mixed[0:count // 2 * 2:2], mixed[1:count // 2 * 2:2]
    margin = jnp.minimum(lengths[donor] - 1, bound - lengths[taker]) // 2
    margin = jnp.where((donor == order[0]) | (taker == order[0]) | (lengths[taker] == 0), 0, jnp.maximum(margin, 0))
    passed = jax.random.randint(jax.random.fold_in(own, 4), (count // 2,), 0, 1 << 20) % (margin + 1)
    lengths = lengths.at[donor].add(-passed).at[taker].add(passed)
    members = jnp.searchsorted(jnp.cumsum(lengths), jnp.arange(rows * top), side="right").astype(jnp.int32)
    listing = members.reshape(top, rows).T
    listing = listing[jax.random.permutation(jax.random.fold_in(own, 1), rows)]
    rotation = jax.random.randint(jax.random.fold_in(own, 2), (rows, 1), 0, top)
    return jnp.take_along_axis(listing, (jnp.arange(top)[None, :] + rotation) % top, axis=1)


def portions_of(amount, total, reach, skew, full):
    portions = [(1 << 20) // math.isqrt(rank ** skew) + 1 for rank in range(1, amount + 1)]
    largest = reach if full else min(reach, max(-(-total // amount), total * portions[0] // sum(portions)))
    least = 1 if total - largest >= amount - 1 else 0
    holding, spare = [largest] + [least] * (amount - 1), total - largest - least * (amount - 1)
    while spare > 0:
        movable = [i for i in range(1, amount) if holding[i] < largest] or [i for i in range(1, amount) if holding[i] < reach]
        pool, remaining = sum([portions[i] for i in movable]), spare
        for i in movable:
            more = min(reach - holding[i], max(1, remaining * portions[i] // pool), spare)
            holding[i] = holding[i] + more
            spare = spare - more
    return np.array(holding)


def normal_values(own_key, extent, scale, most, shards=(), kind=jnp.bfloat16):
    result = scale * jax.random.normal(own_key, extent, jnp.float32)
    if shards:
        result = result * block_levels(own_key, extent, shards, -0.22, 0.18)
    return jnp.clip(result, -most, most).astype(kind)


def setup_inputs(seed: int = 0) -> dict:
    keys = jax.random.split(jax.random.key(seed), 9)
    coupling = normal_values(keys[0], (CHILDREN, BLK, KB * BLK), (KB * BLK) ** -0.5, 0.5, ((0, 16),))
    coupling_pairs = draw_coupling_pairs(jax.random.fold_in(keys[8], 71), 0)
    modes = normal_values(keys[2], (CHILDREN, NBC * BLK, M), 1.0, 6.0, ((0, 16), (2, 2)))
    mode_weights = draw_mode_weights(jax.random.fold_in(keys[8], 71), 0)
    parent_of_keys = jax.random.split(jax.random.fold_in(keys[4], 1), CHILDREN // CH_DEV)
    parent_of_turns = jax.random.permutation(jax.random.fold_in(keys[4], 3), CHILDREN // CH_DEV)
    parent_of = jax.vmap(lambda own, number: deal_out(jax.random.fold_in(keys[4], 2), own, number, CH_DEV, N_SUB, 1, CAPD, 2))(parent_of_keys, parent_of_turns).reshape((CHILDREN, 1))
    row_block = place_ends(jax.random.randint(keys[5], (CHILDREN,), 0, SB), jax.random.fold_in(keys[5], 1), 0, SB - 1).astype(jnp.int32)
    parent_modes = draw_parent_modes(jax.random.fold_in(keys[8], 71), 0)
    parent_eigs = jnp.clip(jnp.exp(math.log(0.5) - 3.218876 * jax.random.uniform(keys[7], (PARENTS, MP), jnp.float32) ** block_levels(keys[7], (PARENTS, MP), ((0, 16),), -0.2, 0.2)), 0.02, 0.5)
    return {"coupling": coupling, "coupling_pairs": coupling_pairs, "modes": modes, "mode_weights": mode_weights, "parent_of": parent_of, "row_block": row_block, "parent_modes": parent_modes, "parent_eigs": parent_eigs}


def reference(coupling, coupling_pairs, modes, mode_weights, parent_of, row_block, parent_modes, parent_eigs):
    parent_blocks = parent_modes.reshape(PARENTS, SB, BLK, MP)

    def projected_of(child):
        picked = modes[child].reshape(NBC, BLK, M)[coupling_pairs[child]].reshape(KB * BLK, M)
        record = jnp.dot(coupling[child].astype(jnp.float32), picked.astype(jnp.float32), preferred_element_type=jnp.float32)
        record = (record * mode_weights[child][None, :].astype(jnp.float32)).astype(jnp.bfloat16)
        parent_rows = parent_blocks[parent_of[child, 0], row_block[child]]
        return jnp.dot(parent_rows.T.astype(jnp.float32), record.astype(jnp.float32), preferred_element_type=jnp.float32).astype(jnp.bfloat16)

    def accumulate(gram_sum, child):
        projected = projected_of(child)
        term = jnp.dot(projected.astype(jnp.float32), projected.T.astype(jnp.float32), preferred_element_type=jnp.float32)
        return (gram_sum.at[parent_of[child, 0]].add(term), None)
    children = jnp.arange(CHILDREN).astype(jnp.int32)
    gram_sum, _ = lax.scan(accumulate, jnp.zeros((PARENTS, MP, MP), jnp.float32), children)
    pencil = gram_sum / (CH_DEV * M) + jax.vmap(jnp.diag)(parent_eigs)
    factor = jnp.linalg.cholesky(pencil)
    identity = jnp.eye(MP, dtype=pencil.dtype)
    inverse = jax.vmap(lambda lower: lax.linalg.triangular_solve(lower, identity, left_side=True, lower=True))(factor).astype(jnp.bfloat16)

    def strength(child):
        projected = projected_of(child)
        rotated = jnp.dot(inverse[parent_of[child, 0]].astype(jnp.float32), projected.astype(jnp.float32), preferred_element_type=jnp.float32)
        return jnp.sum(rotated * rotated, axis=0) / MP
    return lax.map(strength, children)
```

```python
import functools

import jax
import jax.numpy as jnp
from jax import lax
from jax.experimental import pallas as pl
from jax.experimental.pallas import tpu as pltpu
from jax.sharding import PartitionSpec as P

MESH = pl.DeviceIdType.MESH
F32 = jnp.float32
BF16 = jnp.bfloat16
HALVES = 2


def dot(a, b, dims=((1,), (0,)), precision=None):
    return lax.dot_general(a, b, (dims, ((), ())), preferred_element_type=F32, precision=precision)


def exact(a, b, dims=((1,), (0,))):
    return dot(a, b, dims, lax.Precision.HIGHEST)


def split(x, terms):
    parts = []
    for _ in range(terms):
        part = x.astype(BF16)
        parts.append(part)
        x = x - part.astype(F32)
    return parts


def placed(record, right):
    zero = jnp.zeros_like(record)
    return jnp.concatenate(
        [jnp.where(right == 0, record, zero), jnp.where(right == 0, zero, record)], axis=0
    )


def below(block):
    shape = (block, 2 * block)
    row = lax.broadcasted_iota(jnp.int32, shape, 0)
    lane = lax.broadcasted_iota(jnp.int32, shape, 1)
    return row, jnp.where(lane < block, lane, lane - block)


def record_kernel(
    group, parents, parent_of_ref, row_block_ref, pairs_ref,
    coupling_ref, modes_ref, weight_ref, record_ref, pack_ref, gram_ref,
):
    step = pl.program_id(0)

    @pl.when(step == 0)
    def _():
        @pl.loop(0, gram_ref.shape[0])
        def _(i):
            gram_ref[i] = jnp.zeros(gram_ref.shape[1:], F32)

    pairs = pairs_ref.shape[0]
    products = []
    for i in range(group):
        child = step * group + i
        picked = jnp.concatenate(
            [modes_ref[i, pairs_ref[k, child]] for k in range(pairs)], axis=0
        )
        record = dot(coupling_ref[i], picked) * weight_ref[pl.ds(i, 1), :].astype(F32)
        record = record.astype(BF16)
        record_ref[i] = record
        side = row_block_ref[0, child] % 2
        products.append(dot(record, placed(record, side), ((1,), (1,))))
    for i in range(group):
        child = step * group + i
        gram_ref[(row_block_ref[0, child] // 2) * parents + parent_of_ref[0, child]] += products[i]

    @pl.when(step == pl.num_programs(0) - 1)
    def _():
        block = gram_ref.shape[1]
        row, column = below(block)

        @pl.loop(0, parents)
        def _(p):
            for h in range(2):
                upper = gram_ref[h * 2 * parents + p]
                lower = gram_ref[(h * 2 + 1) * parents + p]
                diagonal = jnp.sum(jnp.where(row == column, lower, 0.0), axis=0, keepdims=True)
                pack_ref[h, p, :block] = jnp.where(row <= column, upper, lower)
                pack_ref[h, p, block:] = jnp.broadcast_to(diagonal, (8, 2 * block))


def records_and_grams(parent_of, row_block, pairs, coupling, modes, weights, parents):
    children, block, width = coupling.shape
    columns = modes.shape[2]
    blocks = modes.shape[1] // block
    group = 16
    packed = (2, parents, block + 8, 2 * block)
    return pl.pallas_call(
        functools.partial(record_kernel, group, parents),
        grid_spec=pltpu.PrefetchScalarGridSpec(
            num_scalar_prefetch=3,
            grid=(children // group,),
            in_specs=[
                pl.BlockSpec((group, block, width), lambda i, *_: (i, 0, 0)),
                pl.BlockSpec((group, blocks, block, columns), lambda i, *_: (i, 0, 0, 0)),
                pl.BlockSpec((group, columns), lambda i, *_: (i, 0)),
            ],
            out_specs=[
                pl.BlockSpec((group, block, columns), lambda i, *_: (i, 0, 0)),
                pl.BlockSpec(packed, lambda i, *_: (0, 0, 0, 0)),
            ],
            scratch_shapes=[pltpu.VMEM((4 * parents, block, 2 * block), F32)],
        ),
        out_shape=[
            jax.ShapeDtypeStruct((children, block, columns), BF16),
            jax.ShapeDtypeStruct(packed, F32),
        ],
        name="records",
    )(parent_of, row_block, pairs, coupling, modes.reshape(children, blocks, block, columns), weights)


def eliminate(matrix):
    size, rows, span = matrix.shape[0], 8, 2
    width, count = span * rows, size // rows
    shape = (rows, size)
    lane = lax.broadcasted_iota(jnp.int32, shape, 1)
    row = lax.broadcasted_iota(jnp.int32, shape, 0)

    def spread(x, i):
        return jnp.broadcast_to(x[i : i + 1, :], shape)

    def along(x, i):
        return jnp.broadcast_to(x[:, i : i + 1], shape)

    tiles = [matrix[i * rows : (i + 1) * rows, :] for i in range(count)]
    w, n = [], []
    for g in range(count // span):
        at = g * width
        inside = jnp.logical_and(lane >= at, lane < at + width)
        here = tiles[g * span : (g + 1) * span]
        x = [
            jnp.where(inside, jnp.where(lane - at - i * rows == row, 1.0, 0.0), here[i])
            for i in range(span)
        ]
        w += [jnp.where(lane < at + width, t, 0.0) for t in x]
        columns = [[along(t, at + k) for t in here] for k in range(width)]
        for j in range(0, width, 2):
            h, p, q = j // rows, j % rows, j % rows + 1
            first, second = columns[j], columns[j + 1]
            a, b = spread(first[h], p), spread(second[h], p)
            c, d = spread(first[h], q), spread(second[h], q)
            scale = 1.0 / (a * d - b * c)
            is_p, is_q = row == p, row == q
            pivot = jnp.logical_or(is_p, is_q)
            u = [l * d - r * c for l, r in zip(first, second)]
            v = [r * a - l * b for l, r in zip(first, second)]
            u[h] = jnp.where(is_p, -d, jnp.where(is_q, c, u[h]))
            v[h] = jnp.where(is_p, b, jnp.where(is_q, -a, v[h]))

            def reduced(parts):
                e, f = spread(parts[h], p), spread(parts[h], q)
                base = [jnp.where(pivot, 0.0, t) if i == h else t for i, t in enumerate(parts)]
                return [base[i] - (u[i] * e + v[i] * f) * scale for i in range(span)]

            for k in range(j + 2, width):
                columns[k] = reduced(columns[k])
            x = reduced(x)
        n += [jnp.where(lane < at + width, t, 0.0) for t in x]
        solved = [spread(x[k // rows], k % rows) for k in range(width)]
        for t in range((g + 1) * span, count):
            terms = [along(tiles[t], at + k) * solved[k] for k in range(width)]
            while len(terms) > 1:
                terms = [terms[i] + terms[i + 1] for i in range(0, len(terms), 2)]
            tiles[t] = jnp.where(inside, 0.0, tiles[t]) - terms[0]
    return jnp.concatenate(w, axis=0), jnp.concatenate(n, axis=0)


def halved(packed, diagonal, k):
    row, column = below(packed.shape[0])
    beyond = row < column if k == 0 else row > column
    return jnp.where(beyond, packed, jnp.where(row == column, 0.5 * diagonal, 0.0))


def exchange_kernel(
    subs, scale, parent_of_ref, row_block_ref, gram_ref, record_hbm, parent_ref, eig_ref,
    out_ref,
    record_ref, factor_ref, work, left_ref, right_ref,
    sib, outgoing, recv, tile, packs, spread, record_sem, send_sem, recv_sem,
):
    zs = subs // 4
    me = lax.axis_index("sub")
    core = lax.axis_index("mode")
    z, y, x = me // 4, (me // 2) % 2, me % 2
    offsets = [
        (d, j, i) for d in list(range(1, zs)) + [0] for j in (1, 0) for i in (1, 0) if d or j or i
    ]

    def other(offset):
        d, j, i = offset
        return ((z + d) % zs) * 4 + (y + j) % 2 * 2 + (x + i) % 2

    sibling = (me, 1 - core)
    load = pltpu.make_async_copy(record_hbm, record_ref, record_sem)
    load.start()

    barrier = pltpu.get_barrier_semaphore()
    for peer in [sibling] + [(other(o), core) for o in offsets]:
        pl.semaphore_signal(barrier, inc=1, device_id=peer, device_id_type=MESH)
    pl.semaphore_wait(barrier, subs)

    count = [0]

    def send(src, dst, peer):
        k = count[0]
        count[0] += 1
        copy = pltpu.make_async_remote_copy(
            src_ref=src, dst_ref=dst, send_sem=send_sem.at[k], recv_sem=recv_sem.at[k],
            device_id=peer, device_id_type=MESH,
        )
        copy.start()
        return copy

    block = tile.shape[2] // 2
    order = list(range(1, zs)) + [0]
    swaps = []
    for d in order:
        there = pl.ds(((z + d) % zs) * 4, 4)
        swaps.append(send(gram_ref.at[1 - core, there], sib.at[there], sibling))
    sent = []
    for swap, d in zip(swaps, order):
        swap.wait()
        first = ((z + d) % zs) * 4
        for i in range(4):
            sib[first + i] += gram_ref[core, first + i]
            outgoing[first + i, :block] = sib[first + i, :block].astype(BF16)
            outgoing[first + i, block:] = jnp.broadcast_to(
                sib[first + i, block : block + 1], (16, 2 * block)
            ).astype(BF16)
        for o in offsets:
            if o[0] == d:
                k = (o[0] * 2 + o[1]) * 2 + o[2]
                sent.append((k, send(outgoing.at[other(o)], recv.at[k], (other(o), core))))
    total = sib[me]
    for k, copy in sent:
        copy.wait()
        part = recv[k].astype(F32)
        total = total + part[: block + 8]
    tile[core] = total
    pair = send(tile.at[core], tile.at[core], sibling)

    size = parent_ref.shape[1]
    span = parent_ref.shape[0] // 2
    partial = []
    for h, wait in ((core, False), (1 - core, True)):
        if wait:
            pair.wait()
        packed = tile[h, :block]
        lower = jnp.broadcast_to(tile[h, block : block + 1], packed.shape)
        start = h * span
        for k in range(2):
            terms = split(halved(packed, packed if k == 0 else lower, k), 3)
            for r in range(2):
                at = pl.ds(pl.multiple_of(start + (k * 2 + r) * block, block), block)
                factor_ref[(k * 2 + r) * block : (k * 2 + r + 1) * block, :] = sum(
                    dot(t[:, r * block : (r + 1) * block], parent_ref[at, :]) for t in terms
                )
        rows = parent_ref[pl.ds(pl.multiple_of(start, span), span), :]
        partial.append(sum(dot(rows, t, ((0,), (0,))) for t in split(factor_ref[...], 3)))
    total = partial[0] + partial[1]
    diagonal = lax.broadcasted_iota(jnp.int32, (size, size), 0) == lax.broadcasted_iota(
        jnp.int32, (size, size), 1
    )
    work[...] = jnp.where(diagonal, eig_ref[...], 0.0) + (total + total.T) * scale

    half = size // 2
    nt = ((1,), (1,))
    mine = pl.ds(pl.multiple_of(core * span, span), span)
    front = parent_ref[mine, :half]
    back = parent_ref[mine, half:]
    w, n = eliminate(work[:half, :half])
    ratio = exact(n, work[:half, half:])
    rest = work[half:, half:] - exact(exact(work[half:, :half], w, nt), ratio)
    left_ref[:, :half] = sum(dot(front, t, nt) for t in split(w, 3))
    right_ref[:, :half] = sum(dot(front, t, nt) for t in split(n, 3))
    turned = back.astype(F32) - exact(left_ref[:, :half], ratio)
    w, n = eliminate(rest)
    left_ref[:, half:] = exact(turned, w, nt)
    right_ref[:, half:] = exact(turned, n, nt)
    form = exact(left_ref[...], right_ref[...], nt)
    lane = lax.broadcasted_iota(jnp.int32, (block, 2 * block), 1)
    row, column = below(block)
    forms = []
    for k in range(2):
        at = k * 2 * block
        top = form[at : at + block, at : at + 2 * block]
        bottom = form[at + block : at + 2 * block, at : at + 2 * block]
        forms.append(jnp.where(lane < block, top, bottom))
    diagonal = jnp.sum(jnp.where(row == column, forms[1], 0.0), axis=0, keepdims=True)
    packs[core, me, :block] = jnp.where(row <= column, forms[0], forms[1]).astype(BF16)
    packs[core, me, block:] = jnp.broadcast_to(diagonal, (16, 2 * block)).astype(BF16)

    own = packs.at[core, me]
    sent = [(other(o), send(own, own, (other(o), core))) for o in offsets]

    def unpack(c, s):
        packed = packs[c, s, :block].astype(F32)
        lower = jnp.broadcast_to(packs[c, s, block:].astype(F32)[:1], packed.shape)
        for k in range(2):
            spread[c * 2 + k, s] = halved(packed, packed if k == 0 else lower, k).astype(BF16)

    across = [(me, send(own, own, sibling))]
    unpack(core, me)
    arrive = [((z - o[0]) % zs) * 4 + (y + o[1]) % 2 * 2 + (x + o[2]) % 2 for o in offsets]
    for (_, copy), s in reversed(list(zip(sent, arrive))):
        copy.wait()
        across.append((s, send(packs.at[core, s], packs.at[core, s], sibling)))
        unpack(core, s)
    for s, copy in across:
        copy.wait()
        unpack(1 - core, s)
    load.wait()

    group = 8

    @pl.loop(0, record_ref.shape[0] // group)
    def _(step):
        values = []
        for i in range(group):
            child = step * group + i
            record = record_ref[child]
            parent, place_row = parent_of_ref[0, child], row_block_ref[0, child]
            pushed = dot(spread[place_row // 2, parent], placed(record, place_row % 2))
            values.append(jnp.sum(record.astype(F32) * pushed, axis=0, keepdims=True))
        out_ref[pl.ds(pl.multiple_of(step * group, group), group), :] = (
            jnp.concatenate(values, axis=0) * (2.0 / size)
        )


def strengths(parent_of, row_block, grams, records, parent, eigs, subs, scale):
    children, block, columns = records.shape
    rows, size = parent.shape
    wide = (block + 16, 2 * block)
    copies = subs // 4 + 2 * (subs - 1) + 1 + subs
    vmem = pl.BlockSpec(memory_space=pltpu.VMEM)
    smem = pl.BlockSpec(memory_space=pltpu.SMEM)
    return pl.pallas_call(
        functools.partial(exchange_kernel, subs, scale),
        in_specs=[smem, smem, vmem, pl.BlockSpec(memory_space=pl.ANY), vmem, vmem],
        out_specs=vmem,
        out_shape=jax.ShapeDtypeStruct((children, columns), F32),
        scratch_shapes=[
            pltpu.VMEM(records.shape, BF16),
            pltpu.VMEM((rows // 2, size), F32),
            pltpu.VMEM((size, size), F32),
            pltpu.VMEM((rows // 2, size), F32),
            pltpu.VMEM((rows // 2, size), F32),
            pltpu.VMEM(grams.shape[1:], F32),
            pltpu.VMEM((subs,) + wide, BF16),
            pltpu.VMEM((subs,) + wide, BF16),
            pltpu.VMEM((2,) + grams.shape[2:], F32),
            pltpu.VMEM((2, subs) + wide, BF16),
            pltpu.VMEM((4, subs, block, 2 * block), BF16),
            pltpu.SemaphoreType.DMA,
            pltpu.SemaphoreType.DMA((copies,)),
            pltpu.SemaphoreType.DMA((copies,)),
        ],
        compiler_params=pltpu.CompilerParams(
            collective_id=0, has_side_effects=True, vmem_limit_bytes=60 << 20
        ),
        name="exchange",
    )(parent_of, row_block, grams, records, parent, eigs)


def per_device(
    coupling, coupling_pairs, modes, mode_weights, parent_of, row_block, parent_modes, parent_eigs
):
    subs = lax.axis_size("sub")
    parents = subs * parent_modes.shape[0]
    children = coupling.shape[0]
    parent_of, row_block = parent_of.reshape(1, children), row_block.reshape(1, children)
    records, grams = records_and_grams(
        parent_of, row_block, coupling_pairs.T, coupling, modes, mode_weights, parents
    )
    scale = 1.0 / (children * modes.shape[2] * lax.axis_size("mode"))
    return strengths(
        parent_of, row_block, grams, records, parent_modes[0], parent_eigs, subs, scale
    )


def solution(mesh):
    in_specs = (
        P("sub", None, None),
        P("sub", None),
        P("sub", None, "mode"),
        P("sub", "mode"),
        P("sub", None),
        P("sub"),
        P("sub", None, None),
        P("sub", None),
    )
    return jax.shard_map(
        per_device, mesh=mesh, in_specs=in_specs, out_specs=P("sub", "mode"), check_vma=False
    )
```

```python
import functools

import jax
import jax.numpy as jnp
from jax import lax
from jax.experimental import pallas as pl
from jax.experimental.pallas import tpu as pltpu
from jax.sharding import PartitionSpec as P

MESH = pl.DeviceIdType.MESH
F32 = jnp.float32
BF16 = jnp.bfloat16
HALVES = 2


def dot(a, b, dims=((1,), (0,)), precision=None):
    return lax.dot_general(a, b, (dims, ((), ())), preferred_element_type=F32, precision=precision)


def exact(a, b, dims=((1,), (0,))):
    return dot(a, b, dims, lax.Precision.HIGHEST)


def split(x, terms):
    parts = []
    for _ in range(terms):
        part = x.astype(BF16)
        parts.append(part)
        x = x - part.astype(F32)
    return parts


def placed(record, right):
    zero = jnp.zeros_like(record)
    return jnp.concatenate(
        [jnp.where(right == 0, record, zero), jnp.where(right == 0, zero, record)], axis=0
    )


def below(block):
    shape = (block, 2 * block)
    row = lax.broadcasted_iota(jnp.int32, shape, 0)
    lane = lax.broadcasted_iota(jnp.int32, shape, 1)
    return row, jnp.where(lane < block, lane, lane - block)


def record_kernel(
    group, parents, parent_of_hbm, row_block_hbm, pairs_hbm,
    coupling_hbm, modes_hbm, weight_ref, record_ref, pack_ref,
    parent_of_ref, row_block_ref, pairs_ref, coupling_ref, modes_ref, gram_ref,
    index_sem, coupling_sem, modes_sem,
):
    children, block = record_ref.shape[:2]
    pairs = pairs_ref.shape[0]
    small = [
        pltpu.make_async_copy(src, dst, index_sem.at[k])
        for k, (src, dst) in enumerate(
            [(pairs_hbm, pairs_ref), (row_block_hbm, row_block_ref), (parent_of_hbm, parent_of_ref)]
        )
    ]
    for copy in small:
        copy.start()
    large = []
    for g in range(children // group):
        part = pl.ds(g * group, group)
        pair = [
            pltpu.make_async_copy(coupling_hbm.at[part], coupling_ref.at[part], coupling_sem.at[g]),
            pltpu.make_async_copy(modes_hbm.at[part], modes_ref.at[part], modes_sem.at[g]),
        ]
        for copy in pair:
            copy.start()
        large.append(pair)

    @pl.loop(0, gram_ref.shape[0])
    def _(i):
        gram_ref[i] = jnp.zeros(gram_ref.shape[1:], F32)

    for copy in small:
        copy.wait()
    lane = lax.broadcasted_iota(jnp.int32, (block, 2 * block), 1) // block
    for g in range(children // group):
        for copy in large[g]:
            copy.wait()

        @pl.loop(0, group, step=32)
        def _(start, g=g):
            for first in range(0, 32, 2):
                records = []
                for i in range(2):
                    child = g * group + start + first + i
                    picked = jnp.concatenate(
                        [modes_ref[child, pairs_ref[k, child]] for k in range(pairs)], axis=0
                    )
                    record = dot(coupling_ref[child], picked)
                    record = record * weight_ref[pl.ds(child, 1), :].astype(F32)
                    record = record.astype(BF16)
                    record_ref[child] = record
                    records.append(record)
                stack = jnp.concatenate(records, axis=0)
                product = dot(stack, stack, ((1,), (1,)))
                for i in range(2):
                    child = g * group + start + first + i
                    value = product[i * block : (i + 1) * block]
                    row_block = row_block_ref[0, child]
                    side = row_block % 2
                    value = jnp.where(side == i, value, pltpu.roll(value, block, 1))
                    gram_ref[(row_block // 2) * parents + parent_of_ref[0, child]] += (
                        jnp.where(lane == side, value, 0.0)
                    )

    row, column = below(block)

    @pl.loop(0, parents)
    def _(p):
        for h in range(2):
            upper = gram_ref[h * 2 * parents + p]
            lower = gram_ref[(h * 2 + 1) * parents + p]
            diagonal = jnp.sum(jnp.where(row == column, lower, 0.0), axis=0, keepdims=True)
            pack_ref[h, p, :block] = jnp.where(row <= column, upper, lower)
            pack_ref[h, p, block:] = jnp.broadcast_to(diagonal, (8, 2 * block))


def records_and_grams(parent_of, row_block, pairs, coupling, modes, weights, parents):
    children, block, width = coupling.shape
    columns = modes.shape[2]
    blocks = modes.shape[1] // block
    group = 32
    packed = (2, parents, block + 8, 2 * block)
    modes = modes.reshape(children, blocks, block, columns)
    hbm = pl.BlockSpec(memory_space=pltpu.HBM)
    vmem = pl.BlockSpec(memory_space=pltpu.VMEM)
    coupling, modes, weights, parent_of, row_block, pairs = (
        pltpu.with_memory_space_constraint(a, pltpu.HBM)
        for a in (coupling, modes, weights, parent_of, row_block, pairs)
    )
    return pl.pallas_call(
        functools.partial(record_kernel, group, parents),
        in_specs=[hbm, hbm, hbm, hbm, hbm, vmem],
        out_specs=[vmem, vmem],
        scratch_shapes=[
            pltpu.SMEM(parent_of.shape, jnp.int32),
            pltpu.SMEM(row_block.shape, jnp.int32),
            pltpu.SMEM(pairs.shape, jnp.int32),
            pltpu.VMEM(coupling.shape, BF16),
            pltpu.VMEM(modes.shape, BF16),
            pltpu.VMEM((4 * parents, block, 2 * block), F32),
            pltpu.SemaphoreType.DMA((3,)),
            pltpu.SemaphoreType.DMA((children // group,)),
            pltpu.SemaphoreType.DMA((children // group,)),
        ],
        out_shape=[
            jax.ShapeDtypeStruct((children, block, columns), BF16),
            jax.ShapeDtypeStruct(packed, F32),
        ],
        compiler_params=pltpu.CompilerParams(vmem_limit_bytes=40 << 20),
        name="records",
    )(parent_of, row_block, pairs, coupling, modes, weights)


def eliminate(matrix):
    size, rows, span = matrix.shape[0], 8, 2
    width, count = span * rows, size // rows
    shape = (rows, size)
    lane = lax.broadcasted_iota(jnp.int32, shape, 1)
    row = lax.broadcasted_iota(jnp.int32, shape, 0)

    def spread(x, i):
        return jnp.broadcast_to(x[i : i + 1, :], shape)

    def along(x, i):
        return jnp.broadcast_to(x[:, i : i + 1], shape)

    tiles = [matrix[i * rows : (i + 1) * rows, :] for i in range(count)]
    w, n = [], []
    for g in range(count // span):
        at = g * width
        inside = jnp.logical_and(lane >= at, lane < at + width)
        here = tiles[g * span : (g + 1) * span]
        x = [
            jnp.where(inside, jnp.where(lane - at - i * rows == row, 1.0, 0.0), here[i])
            for i in range(span)
        ]
        w += [jnp.where(lane < at + width, t, 0.0) for t in x]
        columns = [[along(t, at + k) for t in here] for k in range(width)]
        for j in range(0, width, 2):
            h, p, q = j // rows, j % rows, j % rows + 1
            first, second = columns[j], columns[j + 1]
            a, b = spread(first[h], p), spread(second[h], p)
            c, d = spread(first[h], q), spread(second[h], q)
            scale = 1.0 / (a * d - b * c)
            is_p, is_q = row == p, row == q
            pivot = jnp.logical_or(is_p, is_q)
            u = [l * d - r * c for l, r in zip(first, second)]
            v = [r * a - l * b for l, r in zip(first, second)]
            u[h] = jnp.where(is_p, -d, jnp.where(is_q, c, u[h]))
            v[h] = jnp.where(is_p, b, jnp.where(is_q, -a, v[h]))

            def reduced(parts):
                e, f = spread(parts[h], p), spread(parts[h], q)
                base = [jnp.where(pivot, 0.0, t) if i == h else t for i, t in enumerate(parts)]
                return [base[i] - (u[i] * e + v[i] * f) * scale for i in range(span)]

            for k in range(j + 2, width):
                columns[k] = reduced(columns[k])
            x = reduced(x)
        n += [jnp.where(lane < at + width, t, 0.0) for t in x]
        solved = [spread(x[k // rows], k % rows) for k in range(width)]
        for t in range((g + 1) * span, count):
            terms = [along(tiles[t], at + k) * solved[k] for k in range(width)]
            while len(terms) > 1:
                terms = [terms[i] + terms[i + 1] for i in range(0, len(terms), 2)]
            tiles[t] = jnp.where(inside, 0.0, tiles[t]) - terms[0]
    return jnp.concatenate(w, axis=0), jnp.concatenate(n, axis=0)


def halved(packed, diagonal, k):
    row, column = below(packed.shape[0])
    beyond = row < column if k == 0 else row > column
    return jnp.where(beyond, packed, jnp.where(row == column, 0.5 * diagonal, 0.0))


def exchange_kernel(
    subs, scale, parent_of_ref, row_block_ref, gram_ref, record_hbm, parent_ref, eig_ref,
    out_ref,
    record_ref, factor_ref, work, left_ref, right_ref,
    sib, outgoing, recv, tile, packs, spread, record_sem, send_sem, recv_sem,
):
    zs = subs // 4
    me = lax.axis_index("sub")
    core = lax.axis_index("mode")
    z, y, x = me // 4, (me // 2) % 2, me % 2
    offsets = [
        (d, j, i) for d in list(range(1, zs)) + [0] for j in (1, 0) for i in (1, 0) if d or j or i
    ]

    def other(offset):
        d, j, i = offset
        return ((z + d) % zs) * 4 + (y + j) % 2 * 2 + (x + i) % 2

    sibling = (me, 1 - core)
    load = pltpu.make_async_copy(record_hbm, record_ref, record_sem)
    load.start()

    barrier = pltpu.get_barrier_semaphore()
    for peer in [sibling] + [(other(o), core) for o in offsets]:
        pl.semaphore_signal(barrier, inc=1, device_id=peer, device_id_type=MESH)
    pl.semaphore_wait(barrier, subs)

    count = [0]

    def send(src, dst, peer):
        k = count[0]
        count[0] += 1
        copy = pltpu.make_async_remote_copy(
            src_ref=src, dst_ref=dst, send_sem=send_sem.at[k], recv_sem=recv_sem.at[k],
            device_id=peer, device_id_type=MESH,
        )
        copy.start()
        return copy

    block = tile.shape[2] // 2
    order = list(range(1, zs)) + [0]
    swaps = []
    for d in order:
        there = pl.ds(((z + d) % zs) * 4, 4)
        swaps.append(send(gram_ref.at[1 - core, there], sib.at[there], sibling))
    sent = []
    for swap, d in zip(swaps, order):
        swap.wait()
        first = ((z + d) % zs) * 4
        for i in range(4):
            sib[first + i] += gram_ref[core, first + i]
            outgoing[first + i, :block] = sib[first + i, :block].astype(BF16)
            outgoing[first + i, block:] = jnp.broadcast_to(
                sib[first + i, block : block + 1], (16, 2 * block)
            ).astype(BF16)
        for o in offsets:
            if o[0] == d:
                k = (o[0] * 2 + o[1]) * 2 + o[2]
                sent.append((k, send(outgoing.at[other(o)], recv.at[k], (other(o), core))))
    total = sib[me]
    for k, copy in sent:
        copy.wait()
        part = recv[k].astype(F32)
        total = total + part[: block + 8]
    tile[core] = total
    pair = send(tile.at[core], tile.at[core], sibling)

    size = parent_ref.shape[1]
    span = parent_ref.shape[0] // 2
    partial = []
    for h, wait in ((core, False), (1 - core, True)):
        if wait:
            pair.wait()
        packed = tile[h, :block]
        lower = jnp.broadcast_to(tile[h, block : block + 1], packed.shape)
        start = h * span
        for k in range(2):
            terms = split(halved(packed, packed if k == 0 else lower, k), 3)
            for r in range(2):
                at = pl.ds(pl.multiple_of(start + (k * 2 + r) * block, block), block)
                factor_ref[(k * 2 + r) * block : (k * 2 + r + 1) * block, :] = sum(
                    dot(t[:, r * block : (r + 1) * block], parent_ref[at, :]) for t in terms
                )
        rows = parent_ref[pl.ds(pl.multiple_of(start, span), span), :]
        partial.append(sum(dot(rows, t, ((0,), (0,))) for t in split(factor_ref[...], 3)))
    total = partial[0] + partial[1]
    diagonal = lax.broadcasted_iota(jnp.int32, (size, size), 0) == lax.broadcasted_iota(
        jnp.int32, (size, size), 1
    )
    work[...] = jnp.where(diagonal, eig_ref[...], 0.0) + (total + total.T) * scale

    half = size // 2
    nt = ((1,), (1,))
    mine = pl.ds(pl.multiple_of(core * span, span), span)
    front = parent_ref[mine, :half]
    back = parent_ref[mine, half:]
    w, n = eliminate(work[:half, :half])
    ratio = exact(n, work[:half, half:])
    rest = work[half:, half:] - exact(exact(work[half:, :half], w, nt), ratio)
    left_ref[:, :half] = sum(dot(front, t, nt) for t in split(w, 3))
    right_ref[:, :half] = sum(dot(front, t, nt) for t in split(n, 3))
    turned = back.astype(F32) - exact(left_ref[:, :half], ratio)
    w, n = eliminate(rest)
    left_ref[:, half:] = exact(turned, w, nt)
    right_ref[:, half:] = exact(turned, n, nt)
    form = exact(left_ref[...], right_ref[...], nt)
    lane = lax.broadcasted_iota(jnp.int32, (block, 2 * block), 1)
    row, column = below(block)
    forms = []
    for k in range(2):
        at = k * 2 * block
        top = form[at : at + block, at : at + 2 * block]
        bottom = form[at + block : at + 2 * block, at : at + 2 * block]
        forms.append(jnp.where(lane < block, top, bottom))
    diagonal = jnp.sum(jnp.where(row == column, forms[1], 0.0), axis=0, keepdims=True)
    packs[core, me, :block] = jnp.where(row <= column, forms[0], forms[1]).astype(BF16)
    packs[core, me, block:] = jnp.broadcast_to(diagonal, (16, 2 * block)).astype(BF16)

    own = packs.at[core, me]
    sent = [(other(o), send(own, own, (other(o), core))) for o in offsets]

    def unpack(c, s):
        packed = packs[c, s, :block].astype(F32)
        lower = jnp.broadcast_to(packs[c, s, block:].astype(F32)[:1], packed.shape)
        for k in range(2):
            spread[c * 2 + k, s] = halved(packed, packed if k == 0 else lower, k).astype(BF16)

    across = [(me, send(own, own, sibling))]
    unpack(core, me)
    arrive = [((z - o[0]) % zs) * 4 + (y + o[1]) % 2 * 2 + (x + o[2]) % 2 for o in offsets]
    for (_, copy), s in reversed(list(zip(sent, arrive))):
        copy.wait()
        across.append((s, send(packs.at[core, s], packs.at[core, s], sibling)))
        unpack(core, s)
    for s, copy in across:
        copy.wait()
        unpack(1 - core, s)
    load.wait()

    group = 8

    @pl.loop(0, record_ref.shape[0] // group)
    def _(step):
        values = []
        for i in range(group):
            child = step * group + i
            record = record_ref[child]
            parent, place_row = parent_of_ref[0, child], row_block_ref[0, child]
            pushed = dot(spread[place_row // 2, parent], placed(record, place_row % 2))
            values.append(jnp.sum(record.astype(F32) * pushed, axis=0, keepdims=True))
        out_ref[pl.ds(pl.multiple_of(step * group, group), group), :] = (
            jnp.concatenate(values, axis=0) * (2.0 / size)
        )


def strengths(parent_of, row_block, grams, records, parent, eigs, subs, scale):
    children, block, columns = records.shape
    rows, size = parent.shape
    wide = (block + 16, 2 * block)
    copies = subs // 4 + 2 * (subs - 1) + 1 + subs
    vmem = pl.BlockSpec(memory_space=pltpu.VMEM)
    smem = pl.BlockSpec(memory_space=pltpu.SMEM)
    return pl.pallas_call(
        functools.partial(exchange_kernel, subs, scale),
        in_specs=[smem, smem, vmem, pl.BlockSpec(memory_space=pl.ANY), vmem, vmem],
        out_specs=vmem,
        out_shape=jax.ShapeDtypeStruct((children, columns), F32),
        scratch_shapes=[
            pltpu.VMEM(records.shape, BF16),
            pltpu.VMEM((rows // 2, size), F32),
            pltpu.VMEM((size, size), F32),
            pltpu.VMEM((rows // 2, size), F32),
            pltpu.VMEM((rows // 2, size), F32),
            pltpu.VMEM(grams.shape[1:], F32),
            pltpu.VMEM((subs,) + wide, BF16),
            pltpu.VMEM((subs,) + wide, BF16),
            pltpu.VMEM((2,) + grams.shape[2:], F32),
            pltpu.VMEM((2, subs) + wide, BF16),
            pltpu.VMEM((4, subs, block, 2 * block), BF16),
            pltpu.SemaphoreType.DMA,
            pltpu.SemaphoreType.DMA((copies,)),
            pltpu.SemaphoreType.DMA((copies,)),
        ],
        compiler_params=pltpu.CompilerParams(
            collective_id=0, has_side_effects=True, vmem_limit_bytes=32 << 20
        ),
        name="exchange",
    )(parent_of, row_block, grams, records, parent, eigs)


def per_device(
    coupling, coupling_pairs, modes, mode_weights, parent_of, row_block, parent_modes, parent_eigs
):
    subs = lax.axis_size("sub")
    parents = subs * parent_modes.shape[0]
    children = coupling.shape[0]
    parent_of, row_block = parent_of.reshape(1, children), row_block.reshape(1, children)
    records, grams = records_and_grams(
        parent_of, row_block, coupling_pairs.T, coupling, modes, mode_weights, parents
    )
    scale = 1.0 / (children * modes.shape[2] * lax.axis_size("mode"))
    return strengths(
        parent_of, row_block, grams, records, parent_modes[0], parent_eigs, subs, scale
    )


def solution(mesh):
    in_specs = (
        P("sub", None, None),
        P("sub", None),
        P("sub", None, "mode"),
        P("sub", "mode"),
        P("sub", None),
        P("sub"),
        P("sub", None, None),
        P("sub", None),
    )
    return jax.shard_map(
        per_device, mesh=mesh, in_specs=in_specs, out_specs=P("sub", "mode"), check_vma=False
    )
```

```python
import functools

import jax
import jax.numpy as jnp
from jax import lax
from jax.experimental import pallas as pl
from jax.experimental.pallas import tpu as pltpu
from jax.sharding import PartitionSpec as P

MESH = pl.DeviceIdType.MESH
F32 = jnp.float32
BF16 = jnp.bfloat16
HALVES = 2


def dot(a, b, dims=((1,), (0,)), precision=None):
    return lax.dot_general(a, b, (dims, ((), ())), preferred_element_type=F32, precision=precision)


def exact(a, b, dims=((1,), (0,))):
    return dot(a, b, dims, lax.Precision.HIGHEST)


def split(x, terms):
    parts = []
    for _ in range(terms):
        part = x.astype(BF16)
        parts.append(part)
        x = x - part.astype(F32)
    return parts


def placed(record, right):
    zero = jnp.zeros_like(record)
    return jnp.concatenate(
        [jnp.where(right == 0, record, zero), jnp.where(right == 0, zero, record)], axis=0
    )


def below(block):
    shape = (block, 2 * block)
    row = lax.broadcasted_iota(jnp.int32, shape, 0)
    lane = lax.broadcasted_iota(jnp.int32, shape, 1)
    return row, jnp.where(lane < block, lane, lane - block)


def record_kernel(
    group, parents, parent_of_hbm, row_block_hbm, pairs_hbm,
    coupling_hbm, modes_hbm, weight_ref, record_ref, pack_ref,
    parent_of_ref, row_block_ref, pairs_ref, coupling_ref, modes_ref, gram_ref,
    index_sem, coupling_sem, modes_sem,
):
    children, block = record_ref.shape[:2]
    pairs = pairs_ref.shape[0]
    small = [
        pltpu.make_async_copy(src, dst, index_sem.at[k])
        for k, (src, dst) in enumerate(
            [(pairs_hbm, pairs_ref), (row_block_hbm, row_block_ref), (parent_of_hbm, parent_of_ref)]
        )
    ]
    for copy in small:
        copy.start()
    large = []
    for g in range(children // group):
        part = pl.ds(g * group, group)
        pair = [
            pltpu.make_async_copy(coupling_hbm.at[part], coupling_ref.at[part], coupling_sem.at[g]),
            pltpu.make_async_copy(modes_hbm.at[part], modes_ref.at[part], modes_sem.at[g]),
        ]
        for copy in pair:
            copy.start()
        large.append(pair)

    @pl.loop(0, gram_ref.shape[0])
    def _(i):
        gram_ref[i] = jnp.zeros(gram_ref.shape[1:], F32)

    for copy in small:
        copy.wait()
    lane = lax.broadcasted_iota(jnp.int32, (block, 2 * block), 1) // block
    for g in range(children // group):
        for copy in large[g]:
            copy.wait()

        @pl.loop(0, group, step=32)
        def _(start, g=g):
            for first in range(0, 32, 2):
                records = []
                for i in range(2):
                    child = g * group + start + first + i
                    picked = jnp.concatenate(
                        [modes_ref[child, pairs_ref[k, child]] for k in range(pairs)], axis=0
                    )
                    record = dot(coupling_ref[child], picked)
                    record = record * weight_ref[pl.ds(child, 1), :].astype(F32)
                    record = record.astype(BF16)
                    record_ref[child] = record
                    records.append(record)
                stack = jnp.concatenate(records, axis=0)
                product = dot(stack, stack, ((1,), (1,)))
                for i in range(2):
                    child = g * group + start + first + i
                    value = product[i * block : (i + 1) * block]
                    row_block = row_block_ref[0, child]
                    side = row_block % 2
                    value = jnp.where(side == i, value, pltpu.roll(value, block, 1))
                    gram_ref[(row_block // 2) * parents + parent_of_ref[0, child]] += (
                        jnp.where(lane == side, value, 0.0)
                    )

    row, column = below(block)

    @pl.loop(0, parents)
    def _(p):
        for h in range(2):
            upper = gram_ref[h * 2 * parents + p]
            lower = gram_ref[(h * 2 + 1) * parents + p]
            diagonal = jnp.sum(jnp.where(row == column, lower, 0.0), axis=0, keepdims=True)
            pack_ref[h, p, :block] = jnp.where(row <= column, upper, lower)
            pack_ref[h, p, block:] = jnp.broadcast_to(diagonal, (8, 2 * block))


def records_and_grams(parent_of, row_block, pairs, coupling, modes, weights, parents):
    children, block, width = coupling.shape
    columns = modes.shape[2]
    blocks = modes.shape[1] // block
    group = 32
    packed = (2, parents, block + 8, 2 * block)
    modes = modes.reshape(children, blocks, block, columns)
    hbm = pl.BlockSpec(memory_space=pltpu.HBM)
    vmem = pl.BlockSpec(memory_space=pltpu.VMEM)
    coupling, modes, weights, parent_of, row_block, pairs = (
        pltpu.with_memory_space_constraint(a, pltpu.HBM)
        for a in (coupling, modes, weights, parent_of, row_block, pairs)
    )
    return pl.pallas_call(
        functools.partial(record_kernel, group, parents),
        in_specs=[hbm, hbm, hbm, hbm, hbm, vmem],
        out_specs=[vmem, vmem],
        scratch_shapes=[
            pltpu.SMEM(parent_of.shape, jnp.int32),
            pltpu.SMEM(row_block.shape, jnp.int32),
            pltpu.SMEM(pairs.shape, jnp.int32),
            pltpu.VMEM(coupling.shape, BF16),
            pltpu.VMEM(modes.shape, BF16),
            pltpu.VMEM((4 * parents, block, 2 * block), F32),
            pltpu.SemaphoreType.DMA((3,)),
            pltpu.SemaphoreType.DMA((children // group,)),
            pltpu.SemaphoreType.DMA((children // group,)),
        ],
        out_shape=[
            jax.ShapeDtypeStruct((children, block, columns), BF16),
            jax.ShapeDtypeStruct(packed, F32),
        ],
        compiler_params=pltpu.CompilerParams(vmem_limit_bytes=40 << 20),
        name="records",
    )(parent_of, row_block, pairs, coupling, modes, weights)


def eliminate(matrix):
    size, rows, span = matrix.shape[0], 8, 2
    width, count = span * rows, size // rows
    shape = (rows, size)
    lane = lax.broadcasted_iota(jnp.int32, shape, 1)
    row = lax.broadcasted_iota(jnp.int32, shape, 0)

    def spread(x, i):
        return jnp.broadcast_to(x[i : i + 1, :], shape)

    def along(x, i):
        return jnp.broadcast_to(x[:, i : i + 1], shape)

    tiles = [matrix[i * rows : (i + 1) * rows, :] for i in range(count)]
    w, n = [], []
    for g in range(count // span):
        at = g * width
        inside = jnp.logical_and(lane >= at, lane < at + width)
        here = tiles[g * span : (g + 1) * span]
        x = [
            jnp.where(inside, jnp.where(lane - at - i * rows == row, 1.0, 0.0), here[i])
            for i in range(span)
        ]
        w += [jnp.where(lane < at + width, t, 0.0) for t in x]
        columns = [[along(t, at + k) for t in here] for k in range(width)]
        for j in range(0, width, 2):
            h, p, q = j // rows, j % rows, j % rows + 1
            first, second = columns[j], columns[j + 1]
            a, b = spread(first[h], p), spread(second[h], p)
            c, d = spread(first[h], q), spread(second[h], q)
            scale = 1.0 / (a * d - b * c)
            is_p, is_q = row == p, row == q
            pivot = jnp.logical_or(is_p, is_q)
            u = [l * d - r * c for l, r in zip(first, second)]
            v = [r * a - l * b for l, r in zip(first, second)]
            u[h] = jnp.where(is_p, -d, jnp.where(is_q, c, u[h]))
            v[h] = jnp.where(is_p, b, jnp.where(is_q, -a, v[h]))

            def reduced(parts):
                e, f = spread(parts[h], p), spread(parts[h], q)
                base = [jnp.where(pivot, 0.0, t) if i == h else t for i, t in enumerate(parts)]
                return [base[i] - (u[i] * e + v[i] * f) * scale for i in range(span)]

            for k in range(j + 2, width):
                columns[k] = reduced(columns[k])
            x = reduced(x)
        n += [jnp.where(lane < at + width, t, 0.0) for t in x]
        solved = [spread(x[k // rows], k % rows) for k in range(width)]
        for t in range((g + 1) * span, count):
            terms = [along(tiles[t], at + k) * solved[k] for k in range(width)]
            while len(terms) > 1:
                terms = [terms[i] + terms[i + 1] for i in range(0, len(terms), 2)]
            tiles[t] = jnp.where(inside, 0.0, tiles[t]) - terms[0]
    return jnp.concatenate(w, axis=0), jnp.concatenate(n, axis=0)


def halved(packed, diagonal, k):
    row, column = below(packed.shape[0])
    beyond = row < column if k == 0 else row > column
    return jnp.where(beyond, packed, jnp.where(row == column, 0.5 * diagonal, 0.0))


def exchange_kernel(
    subs, scale, parent_of_ref, row_block_ref, gram_ref, record_hbm, parent_ref, eig_ref,
    out_ref,
    record_ref, factor_ref, work, left_ref, right_ref,
    sib, outgoing, ends, recv, recv_ends, tile, packs, pack_ends, spread,
    record_sem, send_sem, recv_sem,
):
    zs = subs // 4
    me = lax.axis_index("sub")
    core = lax.axis_index("mode")
    z, y, x = me // 4, (me // 2) % 2, me % 2
    offsets = [
        (d, j, i) for d in list(range(1, zs)) + [0] for j in (1, 0) for i in (1, 0) if d or j or i
    ]

    def other(offset):
        d, j, i = offset
        return ((z + d) % zs) * 4 + (y + j) % 2 * 2 + (x + i) % 2

    sibling = (me, 1 - core)
    load = pltpu.make_async_copy(record_hbm, record_ref, record_sem)
    load.start()

    barrier = pltpu.get_barrier_semaphore()
    for peer in [sibling] + [(other(o), core) for o in offsets]:
        pl.semaphore_signal(barrier, inc=1, device_id=peer, device_id_type=MESH)
    pl.semaphore_wait(barrier, subs)

    count = [0]

    def send(src, dst, peer):
        k = count[0]
        count[0] += 1
        copy = pltpu.make_async_remote_copy(
            src_ref=src, dst_ref=dst, send_sem=send_sem.at[k], recv_sem=recv_sem.at[k],
            device_id=peer, device_id_type=MESH,
        )
        copy.start()
        return copy

    block = tile.shape[2] // 2
    order = list(range(1, zs)) + [0]
    swaps = []
    for d in order:
        there = pl.ds(((z + d) % zs) * 4, 4)
        swaps.append(send(gram_ref.at[1 - core, there], sib.at[there], sibling))
    sent, small = [], []
    for swap, d in zip(swaps, order):
        swap.wait()
        first = ((z + d) % zs) * 4
        for i in range(4):
            sib[first + i] += gram_ref[core, first + i]
            outgoing[first + i, :block] = sib[first + i, :block].astype(BF16)
            ends[first + i] = sib[first + i, block : block + 1]
        for o in offsets:
            if o[0] == d:
                k = (o[0] * 2 + o[1]) * 2 + o[2]
                target = (other(o), core)
                sent.append((k, send(outgoing.at[other(o)], recv.at[k], target)))
                small.append((k, send(ends.at[other(o)], recv_ends.at[k], target)))
    total, end = sib[me, :block], sib[me, block : block + 1]
    for (k, copy), (_, tail) in zip(sent, small):
        copy.wait()
        tail.wait()
        total = total + recv[k].astype(F32)
        end = end + recv_ends[k]
    tile[core, :block] = total
    tile[core, block:] = jnp.broadcast_to(end, (8, 2 * block))
    pair = send(tile.at[core], tile.at[core], sibling)

    size = parent_ref.shape[1]
    span = parent_ref.shape[0] // 2
    partial = []
    for h, wait in ((core, False), (1 - core, True)):
        if wait:
            pair.wait()
        packed = tile[h, :block]
        lower = jnp.broadcast_to(tile[h, block : block + 1], packed.shape)
        start = h * span
        for k in range(2):
            terms = split(halved(packed, packed if k == 0 else lower, k), 3)
            for r in range(2):
                at = pl.ds(pl.multiple_of(start + (k * 2 + r) * block, block), block)
                factor_ref[(k * 2 + r) * block : (k * 2 + r + 1) * block, :] = sum(
                    dot(t[:, r * block : (r + 1) * block], parent_ref[at, :]) for t in terms
                )
        rows = parent_ref[pl.ds(pl.multiple_of(start, span), span), :]
        partial.append(sum(dot(rows, t, ((0,), (0,))) for t in split(factor_ref[...], 3)))
    total = partial[0] + partial[1]
    diagonal = lax.broadcasted_iota(jnp.int32, (size, size), 0) == lax.broadcasted_iota(
        jnp.int32, (size, size), 1
    )
    work[...] = jnp.where(diagonal, eig_ref[...], 0.0) + (total + total.T) * scale

    half = size // 2
    nt = ((1,), (1,))
    mine = pl.ds(pl.multiple_of(core * span, span), span)
    front = parent_ref[mine, :half]
    back = parent_ref[mine, half:]
    w, n = eliminate(work[:half, :half])
    ratio = exact(n, work[:half, half:])
    rest = work[half:, half:] - exact(exact(work[half:, :half], w, nt), ratio)
    left_ref[:, :half] = sum(dot(front, t, nt) for t in split(w, 3))
    right_ref[:, :half] = sum(dot(front, t, nt) for t in split(n, 3))
    turned = back.astype(F32) - exact(left_ref[:, :half], ratio)
    w, n = eliminate(rest)
    left_ref[:, half:] = exact(turned, w, nt)
    right_ref[:, half:] = exact(turned, n, nt)
    form = exact(left_ref[...], right_ref[...], nt)
    lane = lax.broadcasted_iota(jnp.int32, (block, 2 * block), 1)
    row, column = below(block)
    forms = []
    for k in range(2):
        at = k * 2 * block
        top = form[at : at + block, at : at + 2 * block]
        bottom = form[at + block : at + 2 * block, at : at + 2 * block]
        forms.append(jnp.where(lane < block, top, bottom))
    diagonal = jnp.sum(jnp.where(row == column, forms[1], 0.0), axis=0, keepdims=True)
    packs[core, me] = jnp.where(row <= column, forms[0], forms[1]).astype(BF16)
    pack_ends[core, me] = diagonal

    def both(c, s, peer):
        refs = packs.at[c, s], pack_ends.at[c, s]
        return [send(ref, ref, peer) for ref in refs]

    sent = [both(core, me, (other(o), core)) for o in offsets]

    def unpack(c, s):
        packed = packs[c, s].astype(F32)
        lower = jnp.broadcast_to(pack_ends[c, s], packed.shape)
        for k in range(2):
            spread[c * 2 + k, s] = halved(packed, packed if k == 0 else lower, k).astype(BF16)

    across = [(me, both(core, me, sibling))]
    unpack(core, me)
    arrive = [((z - o[0]) % zs) * 4 + (y + o[1]) % 2 * 2 + (x + o[2]) % 2 for o in offsets]
    for pair, s in reversed(list(zip(sent, arrive))):
        for copy in pair:
            copy.wait()
        across.append((s, both(core, s, sibling)))
        unpack(core, s)
    for s, pair in across:
        for copy in pair:
            copy.wait()
        unpack(1 - core, s)
    load.wait()

    group = 8

    @pl.loop(0, record_ref.shape[0] // group)
    def _(step):
        values = []
        for i in range(group):
            child = step * group + i
            record = record_ref[child]
            parent, place_row = parent_of_ref[0, child], row_block_ref[0, child]
            pushed = dot(spread[place_row // 2, parent], placed(record, place_row % 2))
            values.append(jnp.sum(record.astype(F32) * pushed, axis=0, keepdims=True))
        out_ref[pl.ds(pl.multiple_of(step * group, group), group), :] = (
            jnp.concatenate(values, axis=0) * (2.0 / size)
        )


def strengths(parent_of, row_block, grams, records, parent, eigs, subs, scale):
    children, block, columns = records.shape
    rows, size = parent.shape
    wide, end = (block, 2 * block), (1, 2 * block)
    copies = subs // 4 + 4 * (subs - 1) + 1 + 2 * subs
    vmem = pl.BlockSpec(memory_space=pltpu.VMEM)
    smem = pl.BlockSpec(memory_space=pltpu.SMEM)
    return pl.pallas_call(
        functools.partial(exchange_kernel, subs, scale),
        in_specs=[smem, smem, vmem, pl.BlockSpec(memory_space=pl.ANY), vmem, vmem],
        out_specs=vmem,
        out_shape=jax.ShapeDtypeStruct((children, columns), F32),
        scratch_shapes=[
            pltpu.VMEM(records.shape, BF16),
            pltpu.VMEM((rows // 2, size), F32),
            pltpu.VMEM((size, size), F32),
            pltpu.VMEM((rows // 2, size), F32),
            pltpu.VMEM((rows // 2, size), F32),
            pltpu.VMEM(grams.shape[1:], F32),
            pltpu.VMEM((subs,) + wide, BF16),
            pltpu.VMEM((subs,) + end, F32),
            pltpu.VMEM((subs,) + wide, BF16),
            pltpu.VMEM((subs,) + end, F32),
            pltpu.VMEM((2,) + grams.shape[2:], F32),
            pltpu.VMEM((2, subs) + wide, BF16),
            pltpu.VMEM((2, subs) + end, F32),
            pltpu.VMEM((4, subs, block, 2 * block), BF16),
            pltpu.SemaphoreType.DMA,
            pltpu.SemaphoreType.DMA((copies,)),
            pltpu.SemaphoreType.DMA((copies,)),
        ],
        compiler_params=pltpu.CompilerParams(
            collective_id=0, has_side_effects=True, vmem_limit_bytes=32 << 20
        ),
        name="exchange",
    )(parent_of, row_block, grams, records, parent, eigs)


def per_device(
    coupling, coupling_pairs, modes, mode_weights, parent_of, row_block, parent_modes, parent_eigs
):
    subs = lax.axis_size("sub")
    parents = subs * parent_modes.shape[0]
    children = coupling.shape[0]
    parent_of, row_block = parent_of.reshape(1, children), row_block.reshape(1, children)
    records, grams = records_and_grams(
        parent_of, row_block, coupling_pairs.T, coupling, modes, mode_weights, parents
    )
    scale = 1.0 / (children * modes.shape[2] * lax.axis_size("mode"))
    return strengths(
        parent_of, row_block, grams, records, parent_modes[0], parent_eigs, subs, scale
    )


def solution(mesh):
    in_specs = (
        P("sub", None, None),
        P("sub", None),
        P("sub", None, "mode"),
        P("sub", "mode"),
        P("sub", None),
        P("sub"),
        P("sub", None, None),
        P("sub", None),
    )
    return jax.shard_map(
        per_device, mesh=mesh, in_specs=in_specs, out_specs=P("sub", "mode"), check_vma=False
    )
```

```python
import functools

import jax
import jax.numpy as jnp
from jax import lax
from jax.experimental import pallas as pl
from jax.experimental.pallas import tpu as pltpu
from jax.sharding import PartitionSpec as P

MESH = pl.DeviceIdType.MESH
F32 = jnp.float32
BF16 = jnp.bfloat16
HALVES = 2


def dot(a, b, dims=((1,), (0,)), precision=None):
    return lax.dot_general(a, b, (dims, ((), ())), preferred_element_type=F32, precision=precision)


def exact(a, b, dims=((1,), (0,))):
    return dot(a, b, dims, lax.Precision.HIGHEST)


def split(x, terms):
    parts = []
    for _ in range(terms):
        part = x.astype(BF16)
        parts.append(part)
        x = x - part.astype(F32)
    return parts


def close(a, b, dims):
    (a0, a1), (b0, b1) = split(a, 2), split(b, 2)
    return dot(a0, b0, dims) + (dot(a0, b1, dims) + dot(a1, b0, dims))


def placed(record, right):
    zero = jnp.zeros_like(record)
    return jnp.concatenate(
        [jnp.where(right == 0, record, zero), jnp.where(right == 0, zero, record)], axis=0
    )


def below(block):
    shape = (block, 2 * block)
    row = lax.broadcasted_iota(jnp.int32, shape, 0)
    lane = lax.broadcasted_iota(jnp.int32, shape, 1)
    return row, jnp.where(lane < block, lane, lane - block)


def record_kernel(
    group, parents, parent_of_hbm, row_block_hbm, pairs_hbm,
    coupling_hbm, modes_hbm, weight_hbm, record_ref, pack_ref,
    parent_of_ref, row_block_ref, pairs_ref, weight_ref, coupling_ref, modes_ref, gram_ref,
    index_sem, coupling_sem, modes_sem,
):
    children, block = record_ref.shape[:2]
    pairs = pairs_ref.shape[0]
    small = [
        pltpu.make_async_copy(src, dst, index_sem.at[k])
        for k, (src, dst) in enumerate(
            [
                (pairs_hbm, pairs_ref), (weight_hbm, weight_ref),
                (row_block_hbm, row_block_ref), (parent_of_hbm, parent_of_ref),
            ]
        )
    ]
    for copy in small:
        copy.start()
    large = []
    for g in range(children // group):
        part = pl.ds(g * group, group)
        pair = [
            pltpu.make_async_copy(coupling_hbm.at[part], coupling_ref.at[part], coupling_sem.at[g]),
            pltpu.make_async_copy(modes_hbm.at[part], modes_ref.at[part], modes_sem.at[g]),
        ]
        for copy in pair:
            copy.start()
        large.append(pair)

    @pl.loop(0, gram_ref.shape[0])
    def _(i):
        gram_ref[i] = jnp.zeros(gram_ref.shape[1:], F32)

    for copy in small:
        copy.wait()
    lane = lax.broadcasted_iota(jnp.int32, (block, 2 * block), 1) // block
    for g in range(children // group):
        for copy in large[g]:
            copy.wait()

        @pl.loop(0, group, step=32)
        def _(start, g=g):
            for first in range(0, 32, 2):
                records = []
                for i in range(2):
                    child = g * group + start + first + i
                    picked = jnp.concatenate(
                        [modes_ref[child, pairs_ref[k, child]] for k in range(pairs)], axis=0
                    )
                    record = dot(coupling_ref[child], picked)
                    record = record * weight_ref[pl.ds(child, 1), :].astype(F32)
                    record = record.astype(BF16)
                    record_ref[child] = record
                    records.append(record)
                stack = jnp.concatenate(records, axis=0)
                product = dot(stack, stack, ((1,), (1,)))
                for i in range(2):
                    child = g * group + start + first + i
                    value = product[i * block : (i + 1) * block]
                    row_block = row_block_ref[0, child]
                    side = row_block % 2
                    value = jnp.where(side == i, value, pltpu.roll(value, block, 1))
                    gram_ref[(row_block // 2) * parents + parent_of_ref[0, child]] += (
                        jnp.where(lane == side, value, 0.0)
                    )

    row, column = below(block)

    @pl.loop(0, parents)
    def _(p):
        for h in range(2):
            upper = gram_ref[h * 2 * parents + p]
            lower = gram_ref[(h * 2 + 1) * parents + p]
            diagonal = jnp.sum(jnp.where(row == column, lower, 0.0), axis=0, keepdims=True)
            pack_ref[h, p, :block] = jnp.where(row <= column, upper, lower)
            pack_ref[h, p, block:] = jnp.broadcast_to(diagonal, (8, 2 * block))


def records_and_grams(parent_of, row_block, pairs, coupling, modes, weights, parents):
    children, block, width = coupling.shape
    columns = modes.shape[2]
    blocks = modes.shape[1] // block
    group = 32
    packed = (2, parents, block + 8, 2 * block)
    modes = modes.reshape(children, blocks, block, columns)
    hbm = pl.BlockSpec(memory_space=pltpu.HBM)
    vmem = pl.BlockSpec(memory_space=pltpu.VMEM)
    coupling, modes, weights, parent_of, row_block, pairs = (
        pltpu.with_memory_space_constraint(a, pltpu.HBM)
        for a in (coupling, modes, weights, parent_of, row_block, pairs)
    )
    return pl.pallas_call(
        functools.partial(record_kernel, group, parents),
        in_specs=[hbm] * 6,
        out_specs=[vmem, vmem],
        scratch_shapes=[
            pltpu.SMEM(parent_of.shape, jnp.int32),
            pltpu.SMEM(row_block.shape, jnp.int32),
            pltpu.SMEM(pairs.shape, jnp.int32),
            pltpu.VMEM(weights.shape, BF16),
            pltpu.VMEM(coupling.shape, BF16),
            pltpu.VMEM(modes.shape, BF16),
            pltpu.VMEM((4 * parents, block, 2 * block), F32),
            pltpu.SemaphoreType.DMA((4,)),
            pltpu.SemaphoreType.DMA((children // group,)),
            pltpu.SemaphoreType.DMA((children // group,)),
        ],
        out_shape=[
            jax.ShapeDtypeStruct((children, block, columns), BF16),
            jax.ShapeDtypeStruct(packed, F32),
        ],
        compiler_params=pltpu.CompilerParams(vmem_limit_bytes=40 << 20),
        name="records",
    )(parent_of, row_block, pairs, coupling, modes, weights)


def eliminate(matrix):
    size, rows, span = matrix.shape[0], 8, 2
    width, count = span * rows, size // rows
    shape = (rows, size)
    lane = lax.broadcasted_iota(jnp.int32, shape, 1)
    row = lax.broadcasted_iota(jnp.int32, shape, 0)

    def spread(x, i):
        return jnp.broadcast_to(x[i : i + 1, :], shape)

    def along(x, i):
        return jnp.broadcast_to(x[:, i : i + 1], shape)

    tiles = [matrix[i * rows : (i + 1) * rows, :] for i in range(count)]
    w, n = [], []
    for g in range(count // span):
        at = g * width
        inside = jnp.logical_and(lane >= at, lane < at + width)
        here = tiles[g * span : (g + 1) * span]
        x = [
            jnp.where(inside, jnp.where(lane - at - i * rows == row, 1.0, 0.0), here[i])
            for i in range(span)
        ]
        w += [jnp.where(lane < at + width, t, 0.0) for t in x]
        columns = [[along(t, at + k) for t in here] for k in range(width)]
        for j in range(0, width, 2):
            h, p, q = j // rows, j % rows, j % rows + 1
            first, second = columns[j], columns[j + 1]
            a, b = spread(first[h], p), spread(second[h], p)
            c, d = spread(first[h], q), spread(second[h], q)
            scale = 1.0 / (a * d - b * c)
            is_p, is_q = row == p, row == q
            pivot = jnp.logical_or(is_p, is_q)
            u = [l * d - r * c for l, r in zip(first, second)]
            v = [r * a - l * b for l, r in zip(first, second)]
            u[h] = jnp.where(is_p, -d, jnp.where(is_q, c, u[h]))
            v[h] = jnp.where(is_p, b, jnp.where(is_q, -a, v[h]))

            def reduced(parts):
                e, f = spread(parts[h], p), spread(parts[h], q)
                base = [jnp.where(pivot, 0.0, t) if i == h else t for i, t in enumerate(parts)]
                return [base[i] - (u[i] * e + v[i] * f) * scale for i in range(span)]

            for k in range(j + 2, width):
                columns[k] = reduced(columns[k])
            x = reduced(x)
        n += [jnp.where(lane < at + width, t, 0.0) for t in x]
        solved = [spread(x[k // rows], k % rows) for k in range(width)]
        for t in range((g + 1) * span, count):
            terms = [along(tiles[t], at + k) * solved[k] for k in range(width)]
            while len(terms) > 1:
                terms = [terms[i] + terms[i + 1] for i in range(0, len(terms), 2)]
            tiles[t] = jnp.where(inside, 0.0, tiles[t]) - terms[0]
    return jnp.concatenate(w, axis=0), jnp.concatenate(n, axis=0)


def halved(packed, diagonal, k):
    row, column = below(packed.shape[0])
    beyond = row < column if k == 0 else row > column
    return jnp.where(beyond, packed, jnp.where(row == column, 0.5 * diagonal, 0.0))


def exchange_kernel(
    subs, scale, parent_of_ref, row_block_ref, gram_ref, record_hbm, parent_ref, eig_ref,
    out_ref,
    record_ref, factor_ref, work, left_ref, right_ref,
    sib, outgoing, ends, recv, recv_ends, tile, packs, pack_ends, spread,
    record_sem, send_sem, recv_sem,
):
    zs = subs // 4
    me = lax.axis_index("sub")
    core = lax.axis_index("mode")
    z, y, x = me // 4, (me // 2) % 2, me % 2
    offsets = [
        (d, j, i) for d in list(range(1, zs)) + [0] for j in (1, 0) for i in (1, 0) if d or j or i
    ]

    def other(offset):
        d, j, i = offset
        return ((z + d) % zs) * 4 + (y + j) % 2 * 2 + (x + i) % 2

    sibling = (me, 1 - core)
    load = pltpu.make_async_copy(record_hbm, record_ref, record_sem)
    load.start()

    barrier = pltpu.get_barrier_semaphore()
    for peer in [sibling] + [(other(o), core) for o in offsets]:
        pl.semaphore_signal(barrier, inc=1, device_id=peer, device_id_type=MESH)
    pl.semaphore_wait(barrier, subs)

    count = [0]

    def send(src, dst, peer):
        k = count[0]
        count[0] += 1
        copy = pltpu.make_async_remote_copy(
            src_ref=src, dst_ref=dst, send_sem=send_sem.at[k], recv_sem=recv_sem.at[k],
            device_id=peer, device_id_type=MESH,
        )
        copy.start()
        return copy

    block = tile.shape[2] // 2
    order = list(range(1, zs)) + [0]
    swaps = []
    for d in order:
        there = pl.ds(((z + d) % zs) * 4, 4)
        swaps.append(send(gram_ref.at[1 - core, there], sib.at[there], sibling))
    sent, small = [], []
    for swap, d in zip(swaps, order):
        swap.wait()
        first = ((z + d) % zs) * 4
        for i in range(4):
            sib[first + i] += gram_ref[core, first + i]
            outgoing[first + i, :block] = sib[first + i, :block].astype(BF16)
            ends[first + i] = sib[first + i, block : block + 1]
        for o in offsets:
            if o[0] == d:
                k = (o[0] * 2 + o[1]) * 2 + o[2]
                target = (other(o), core)
                sent.append((k, send(outgoing.at[other(o)], recv.at[k], target)))
                small.append((k, send(ends.at[other(o)], recv_ends.at[k], target)))
    total, end = sib[me, :block], sib[me, block : block + 1]
    for (k, copy), (_, tail) in zip(sent, small):
        copy.wait()
        tail.wait()
        total = total + recv[k].astype(F32)
        end = end + recv_ends[k]
    tile[core, :block] = total
    tile[core, block:] = jnp.broadcast_to(end, (8, 2 * block))
    pair = send(tile.at[core], tile.at[core], sibling)

    size = parent_ref.shape[1]
    span = parent_ref.shape[0] // 2
    partial = []
    for h, wait in ((core, False), (1 - core, True)):
        if wait:
            pair.wait()
        packed = tile[h, :block]
        lower = jnp.broadcast_to(tile[h, block : block + 1], packed.shape)
        start = h * span
        for k in range(2):
            terms = split(halved(packed, packed if k == 0 else lower, k), 3)
            for r in range(2):
                at = pl.ds(pl.multiple_of(start + (k * 2 + r) * block, block), block)
                factor_ref[(k * 2 + r) * block : (k * 2 + r + 1) * block, :] = sum(
                    dot(t[:, r * block : (r + 1) * block], parent_ref[at, :]) for t in terms
                )
        rows = parent_ref[pl.ds(pl.multiple_of(start, span), span), :]
        partial.append(sum(dot(rows, t, ((0,), (0,))) for t in split(factor_ref[...], 3)))
    total = partial[0] + partial[1]
    diagonal = lax.broadcasted_iota(jnp.int32, (size, size), 0) == lax.broadcasted_iota(
        jnp.int32, (size, size), 1
    )
    work[...] = jnp.where(diagonal, eig_ref[...], 0.0) + (total + total.T) * scale

    half = size // 2
    nt = ((1,), (1,))
    mine = pl.ds(pl.multiple_of(core * span, span), span)
    front = parent_ref[mine, :half]
    back = parent_ref[mine, half:]
    w, n = eliminate(work[:half, :half])
    ratio = exact(n, work[:half, half:])
    rest = work[half:, half:] - exact(exact(work[half:, :half], w, nt), ratio)
    left_ref[:, :half] = sum(dot(front, t, nt) for t in split(w, 3))
    right_ref[:, :half] = sum(dot(front, t, nt) for t in split(n, 2))
    turned = back.astype(F32) - exact(left_ref[:, :half], ratio)
    w, n = eliminate(rest)
    left_ref[:, half:] = close(turned, w, nt)
    right_ref[:, half:] = close(turned, n, nt)
    form = close(left_ref[...], right_ref[...], nt)
    lane = lax.broadcasted_iota(jnp.int32, (block, 2 * block), 1)
    row, column = below(block)
    forms = []
    for k in range(2):
        at = k * 2 * block
        top = form[at : at + block, at : at + 2 * block]
        bottom = form[at + block : at + 2 * block, at : at + 2 * block]
        forms.append(jnp.where(lane < block, top, bottom))
    diagonal = jnp.sum(jnp.where(row == column, forms[1], 0.0), axis=0, keepdims=True)
    packs[core, me] = jnp.where(row <= column, forms[0], forms[1]).astype(BF16)
    pack_ends[core, me] = diagonal

    def both(c, s, peer):
        refs = packs.at[c, s], pack_ends.at[c, s]
        return [send(ref, ref, peer) for ref in refs]

    sent = [both(core, me, (other(o), core)) for o in offsets]

    def unpack(c, s):
        packed = packs[c, s].astype(F32)
        lower = jnp.broadcast_to(pack_ends[c, s], packed.shape)
        for k in range(2):
            spread[c * 2 + k, s] = halved(packed, packed if k == 0 else lower, k).astype(BF16)

    across = [(me, both(core, me, sibling))]
    unpack(core, me)
    arrive = [((z - o[0]) % zs) * 4 + (y + o[1]) % 2 * 2 + (x + o[2]) % 2 for o in offsets]
    for pair, s in reversed(list(zip(sent, arrive))):
        for copy in pair:
            copy.wait()
        across.append((s, both(core, s, sibling)))
        unpack(core, s)
    for s, pair in across:
        for copy in pair:
            copy.wait()
        unpack(1 - core, s)
    load.wait()

    group = 32

    @pl.loop(0, record_ref.shape[0] // group)
    def _(step):
        values = []
        for i in range(group):
            child = step * group + i
            record = record_ref[child]
            parent, place_row = parent_of_ref[0, child], row_block_ref[0, child]
            pushed = dot(spread[place_row // 2, parent], placed(record, place_row % 2))
            values.append(jnp.sum(record.astype(F32) * pushed, axis=0, keepdims=True))
        out_ref[pl.ds(pl.multiple_of(step * group, group), group), :] = (
            jnp.concatenate(values, axis=0) * (2.0 / size)
        )


def strengths(parent_of, row_block, grams, records, parent, eigs, subs, scale):
    children, block, columns = records.shape
    rows, size = parent.shape
    wide, end = (block, 2 * block), (1, 2 * block)
    copies = subs // 4 + 4 * (subs - 1) + 1 + 2 * subs
    vmem = pl.BlockSpec(memory_space=pltpu.VMEM)
    smem = pl.BlockSpec(memory_space=pltpu.SMEM)
    return pl.pallas_call(
        functools.partial(exchange_kernel, subs, scale),
        in_specs=[smem, smem, vmem, pl.BlockSpec(memory_space=pl.ANY), vmem, vmem],
        out_specs=vmem,
        out_shape=jax.ShapeDtypeStruct((children, columns), F32),
        scratch_shapes=[
            pltpu.VMEM(records.shape, BF16),
            pltpu.VMEM((rows // 2, size), F32),
            pltpu.VMEM((size, size), F32),
            pltpu.VMEM((rows // 2, size), F32),
            pltpu.VMEM((rows // 2, size), F32),
            pltpu.VMEM(grams.shape[1:], F32),
            pltpu.VMEM((subs,) + wide, BF16),
            pltpu.VMEM((subs,) + end, F32),
            pltpu.VMEM((subs,) + wide, BF16),
            pltpu.VMEM((subs,) + end, F32),
            pltpu.VMEM((2,) + grams.shape[2:], F32),
            pltpu.VMEM((2, subs) + wide, BF16),
            pltpu.VMEM((2, subs) + end, F32),
            pltpu.VMEM((4, subs, block, 2 * block), BF16),
            pltpu.SemaphoreType.DMA,
            pltpu.SemaphoreType.DMA((copies,)),
            pltpu.SemaphoreType.DMA((copies,)),
        ],
        compiler_params=pltpu.CompilerParams(
            collective_id=0, has_side_effects=True, vmem_limit_bytes=32 << 20
        ),
        name="exchange",
    )(parent_of, row_block, grams, records, parent, eigs)


def per_device(
    coupling, coupling_pairs, modes, mode_weights, parent_of, row_block, parent_modes, parent_eigs
):
    subs = lax.axis_size("sub")
    parents = subs * parent_modes.shape[0]
    children = coupling.shape[0]
    parent_of, row_block = parent_of.reshape(1, children), row_block.reshape(1, children)
    records, grams = records_and_grams(
        parent_of, row_block, coupling_pairs.T, coupling, modes, mode_weights, parents
    )
    scale = 1.0 / (children * modes.shape[2] * lax.axis_size("mode"))
    return strengths(
        parent_of, row_block, grams, records, parent_modes[0], parent_eigs, subs, scale
    )


def solution(mesh):
    in_specs = (
        P("sub", None, None),
        P("sub", None),
        P("sub", None, "mode"),
        P("sub", "mode"),
        P("sub", None),
        P("sub"),
        P("sub", None, None),
        P("sub", None),
    )
    return jax.shard_map(
        per_device, mesh=mesh, in_specs=in_specs, out_specs=P("sub", "mode"), check_vma=False
    )
```

```python
import functools

import jax
import jax.numpy as jnp
from jax import lax
from jax.experimental import pallas as pl
from jax.experimental.pallas import tpu as pltpu
from jax.sharding import PartitionSpec as P

MESH = pl.DeviceIdType.MESH
F32 = jnp.float32
BF16 = jnp.bfloat16
HALVES = 2


def dot(a, b, dims=((1,), (0,)), precision=None):
    return lax.dot_general(a, b, (dims, ((), ())), preferred_element_type=F32, precision=precision)


def exact(a, b, dims=((1,), (0,))):
    return dot(a, b, dims, lax.Precision.HIGHEST)


def split(x, terms):
    parts = []
    for _ in range(terms):
        part = x.astype(BF16)
        parts.append(part)
        x = x - part.astype(F32)
    return parts


def close(a, b, dims):
    (a0, a1), (b0, b1) = split(a, 2), split(b, 2)
    return dot(a0, b0, dims) + (dot(a0, b1, dims) + dot(a1, b0, dims))


def placed(record, right):
    zero = jnp.zeros_like(record)
    return jnp.concatenate(
        [jnp.where(right == 0, record, zero), jnp.where(right == 0, zero, record)], axis=0
    )


def below(block):
    shape = (block, 2 * block)
    row = lax.broadcasted_iota(jnp.int32, shape, 0)
    lane = lax.broadcasted_iota(jnp.int32, shape, 1)
    return row, jnp.where(lane < block, lane, lane - block)


def record_kernel(
    group, parents, parent_of_hbm, row_block_hbm, pairs_hbm,
    coupling_hbm, modes_hbm, weight_hbm, record_ref, gram_ref,
    parent_of_ref, row_block_ref, pairs_ref, weight_ref, coupling_ref, modes_ref,
    index_sem, coupling_sem, modes_sem,
):
    children, block = record_ref.shape[:2]
    pairs = pairs_ref.shape[0]
    small = [
        pltpu.make_async_copy(src, dst, index_sem.at[k])
        for k, (src, dst) in enumerate(
            [
                (pairs_hbm, pairs_ref), (weight_hbm, weight_ref),
                (row_block_hbm, row_block_ref), (parent_of_hbm, parent_of_ref),
            ]
        )
    ]
    for copy in small:
        copy.start()
    large = []
    for g in range(children // group):
        part = pl.ds(g * group, group)
        pair = [
            pltpu.make_async_copy(coupling_hbm.at[part], coupling_ref.at[part], coupling_sem.at[g]),
            pltpu.make_async_copy(modes_hbm.at[part], modes_ref.at[part], modes_sem.at[g]),
        ]
        for copy in pair:
            copy.start()
        large.append(pair)

    @pl.loop(0, gram_ref.shape[0])
    def _(i):
        gram_ref[i] = jnp.zeros(gram_ref.shape[1:], F32)

    for copy in small:
        copy.wait()
    lane = lax.broadcasted_iota(jnp.int32, (block, 2 * block), 1) // block
    for g in range(children // group):
        for copy in large[g]:
            copy.wait()

        @pl.loop(0, group, step=32)
        def _(start, g=g):
            for first in range(0, 32, 2):
                records = []
                for i in range(2):
                    child = g * group + start + first + i
                    picked = jnp.concatenate(
                        [modes_ref[child, pairs_ref[k, child]] for k in range(pairs)], axis=0
                    )
                    record = dot(coupling_ref[child], picked)
                    record = record * weight_ref[pl.ds(child, 1), :].astype(F32)
                    record = record.astype(BF16)
                    record_ref[child] = record
                    records.append(record)
                stack = jnp.concatenate(records, axis=0)
                product = dot(stack, stack, ((1,), (1,)))
                for i in range(2):
                    child = g * group + start + first + i
                    value = product[i * block : (i + 1) * block]
                    row_block = row_block_ref[0, child]
                    side = row_block % 2
                    value = jnp.where(side == i, value, pltpu.roll(value, block, 1))
                    gram_ref[(row_block // 2) * parents + parent_of_ref[0, child]] += (
                        jnp.where(lane == side, value, 0.0)
                    )


def records_and_grams(parent_of, row_block, pairs, coupling, modes, weights, parents):
    children, block, width = coupling.shape
    columns = modes.shape[2]
    blocks = modes.shape[1] // block
    group = 32
    modes = modes.reshape(children, blocks, block, columns)
    hbm = pl.BlockSpec(memory_space=pltpu.HBM)
    vmem = pl.BlockSpec(memory_space=pltpu.VMEM)
    coupling, modes, weights, parent_of, row_block, pairs = (
        pltpu.with_memory_space_constraint(a, pltpu.HBM)
        for a in (coupling, modes, weights, parent_of, row_block, pairs)
    )
    return pl.pallas_call(
        functools.partial(record_kernel, group, parents),
        in_specs=[hbm] * 6,
        out_specs=[vmem, vmem],
        scratch_shapes=[
            pltpu.SMEM(parent_of.shape, jnp.int32),
            pltpu.SMEM(row_block.shape, jnp.int32),
            pltpu.SMEM(pairs.shape, jnp.int32),
            pltpu.VMEM(weights.shape, BF16),
            pltpu.VMEM(coupling.shape, BF16),
            pltpu.VMEM(modes.shape, BF16),
            pltpu.SemaphoreType.DMA((4,)),
            pltpu.SemaphoreType.DMA((children // group,)),
            pltpu.SemaphoreType.DMA((children // group,)),
        ],
        out_shape=[
            jax.ShapeDtypeStruct((children, block, columns), BF16),
            jax.ShapeDtypeStruct((4 * parents, block, 2 * block), F32),
        ],
        compiler_params=pltpu.CompilerParams(vmem_limit_bytes=40 << 20),
        name="records",
    )(parent_of, row_block, pairs, coupling, modes, weights)


def eliminate(matrix):
    size, rows, span = matrix.shape[0], 8, 2
    width, count = span * rows, size // rows
    shape = (rows, size)
    lane = lax.broadcasted_iota(jnp.int32, shape, 1)
    row = lax.broadcasted_iota(jnp.int32, shape, 0)

    def spread(x, i):
        return jnp.broadcast_to(x[i : i + 1, :], shape)

    def along(x, i):
        return jnp.broadcast_to(x[:, i : i + 1], shape)

    tiles = [matrix[i * rows : (i + 1) * rows, :] for i in range(count)]
    w, n = [], []
    for g in range(count // span):
        at = g * width
        inside = jnp.logical_and(lane >= at, lane < at + width)
        here = tiles[g * span : (g + 1) * span]
        x = [
            jnp.where(inside, jnp.where(lane - at - i * rows == row, 1.0, 0.0), here[i])
            for i in range(span)
        ]
        w += [jnp.where(lane < at + width, t, 0.0) for t in x]
        columns = [[along(t, at + k) for t in here] for k in range(width)]
        for j in range(0, width, 2):
            h, p, q = j // rows, j % rows, j % rows + 1
            first, second = columns[j], columns[j + 1]
            a, b = spread(first[h], p), spread(second[h], p)
            c, d = spread(first[h], q), spread(second[h], q)
            scale = 1.0 / (a * d - b * c)
            is_p, is_q = row == p, row == q
            pivot = jnp.logical_or(is_p, is_q)
            u = [l * d - r * c for l, r in zip(first, second)]
            v = [r * a - l * b for l, r in zip(first, second)]
            u[h] = jnp.where(is_p, -d, jnp.where(is_q, c, u[h]))
            v[h] = jnp.where(is_p, b, jnp.where(is_q, -a, v[h]))

            def reduced(parts):
                e, f = spread(parts[h], p), spread(parts[h], q)
                base = [jnp.where(pivot, 0.0, t) if i == h else t for i, t in enumerate(parts)]
                return [base[i] - (u[i] * e + v[i] * f) * scale for i in range(span)]

            for k in range(j + 2, width):
                columns[k] = reduced(columns[k])
            x = reduced(x)
        n += [jnp.where(lane < at + width, t, 0.0) for t in x]
        solved = [spread(x[k // rows], k % rows) for k in range(width)]
        for t in range((g + 1) * span, count):
            terms = [along(tiles[t], at + k) * solved[k] for k in range(width)]
            while len(terms) > 1:
                terms = [terms[i] + terms[i + 1] for i in range(0, len(terms), 2)]
            tiles[t] = jnp.where(inside, 0.0, tiles[t]) - terms[0]
    return jnp.concatenate(w, axis=0), jnp.concatenate(n, axis=0)


def halved(packed, diagonal, k):
    row, column = below(packed.shape[0])
    beyond = row < column if k == 0 else row > column
    return jnp.where(beyond, packed, jnp.where(row == column, 0.5 * diagonal, 0.0))


def exchange_kernel(
    subs, scale, parent_of_ref, row_block_ref, gram_ref, record_hbm, parent_ref, eig_ref,
    out_ref,
    record_ref, factor_ref, work, left_ref, right_ref,
    mine, mine_ends, give, give_ends, sib, sib_ends, outgoing, ends, recv, recv_ends, tile, packs, pack_ends, spread,
    record_sem, send_sem, recv_sem,
):
    zs = subs // 4
    me = lax.axis_index("sub")
    core = lax.axis_index("mode")
    z, y, x = me // 4, (me // 2) % 2, me % 2
    offsets = [
        (d, j, i) for d in list(range(1, zs)) + [0] for j in (1, 0) for i in (1, 0) if d or j or i
    ]

    def other(offset):
        d, j, i = offset
        return ((z + d) % zs) * 4 + (y + j) % 2 * 2 + (x + i) % 2

    sibling = (me, 1 - core)
    load = pltpu.make_async_copy(record_hbm, record_ref, record_sem)
    load.start()

    barrier = pltpu.get_barrier_semaphore()
    for peer in [sibling] + [(other(o), core) for o in offsets]:
        pl.semaphore_signal(barrier, inc=1, device_id=peer, device_id_type=MESH)
    block = tile.shape[2] // 2
    row, column = below(block)

    @pl.loop(0, subs)
    def _(p):
        for h, own in ((core, True), (1 - core, False)):
            upper = gram_ref[h * 2 * subs + p]
            lower = gram_ref[(h * 2 + 1) * subs + p]
            end = jnp.sum(jnp.where(row == column, lower, 0.0), axis=0, keepdims=True)
            packed = jnp.where(row <= column, upper, lower)
            if own:
                mine[p] = packed
                mine_ends[p] = end
            else:
                give[p] = packed.astype(BF16)
                give_ends[p] = end

    pl.semaphore_wait(barrier, subs)

    count = [0]

    def send(src, dst, peer):
        k = count[0]
        count[0] += 1
        copy = pltpu.make_async_remote_copy(
            src_ref=src, dst_ref=dst, send_sem=send_sem.at[k], recv_sem=recv_sem.at[k],
            device_id=peer, device_id_type=MESH,
        )
        copy.start()
        return copy

    order = list(range(1, zs)) + [0]
    swaps = []
    for d in order:
        there = pl.ds(((z + d) % zs) * 4, 4)
        swaps.append(
            [
                send(give.at[there], sib.at[there], sibling),
                send(give_ends.at[there], sib_ends.at[there], sibling),
            ]
        )
    sent, small = [], []
    for swap, d in zip(swaps, order):
        for copy in swap:
            copy.wait()
        first = ((z + d) % zs) * 4
        for i in range(4):
            summed = mine[first + i] + sib[first + i].astype(F32)
            mine[first + i] = summed
            outgoing[first + i] = summed.astype(BF16)
            ends[first + i] = mine_ends[first + i] + sib_ends[first + i]
        for o in offsets:
            if o[0] == d:
                k = (o[0] * 2 + o[1]) * 2 + o[2]
                target = (other(o), core)
                sent.append((k, send(outgoing.at[other(o)], recv.at[k], target)))
                small.append((k, send(ends.at[other(o)], recv_ends.at[k], target)))
    total, end = mine[me], ends[me]
    for (k, copy), (_, tail) in zip(sent, small):
        copy.wait()
        tail.wait()
        total = total + recv[k].astype(F32)
        end = end + recv_ends[k]
    tile[core, :block] = total
    tile[core, block:] = jnp.broadcast_to(end, (8, 2 * block))
    pair = send(tile.at[core], tile.at[core], sibling)

    size = parent_ref.shape[1]
    span = parent_ref.shape[0] // 2
    partial = []
    for h, wait in ((core, False), (1 - core, True)):
        if wait:
            pair.wait()
        packed = tile[h, :block]
        lower = jnp.broadcast_to(tile[h, block : block + 1], packed.shape)
        start = h * span
        for k in range(2):
            terms = split(halved(packed, packed if k == 0 else lower, k), 3)
            for r in range(2):
                at = pl.ds(pl.multiple_of(start + (k * 2 + r) * block, block), block)
                factor_ref[(k * 2 + r) * block : (k * 2 + r + 1) * block, :] = sum(
                    dot(t[:, r * block : (r + 1) * block], parent_ref[at, :]) for t in terms
                )
        rows = parent_ref[pl.ds(pl.multiple_of(start, span), span), :]
        partial.append(sum(dot(rows, t, ((0,), (0,))) for t in split(factor_ref[...], 3)))
    total = partial[0] + partial[1]
    diagonal = lax.broadcasted_iota(jnp.int32, (size, size), 0) == lax.broadcasted_iota(
        jnp.int32, (size, size), 1
    )
    work[...] = jnp.where(diagonal, eig_ref[...], 0.0) + (total + total.T) * scale

    half = size // 2
    nt = ((1,), (1,))
    mine = pl.ds(pl.multiple_of(core * span, span), span)
    front = parent_ref[mine, :half]
    back = parent_ref[mine, half:]
    w, n = eliminate(work[:half, :half])
    ratio = exact(n, work[:half, half:])
    rest = work[half:, half:] - exact(exact(work[half:, :half], w, nt), ratio)
    left_ref[:, :half] = sum(dot(front, t, nt) for t in split(w, 3))
    right_ref[:, :half] = sum(dot(front, t, nt) for t in split(n, 2))
    turned = back.astype(F32) - exact(left_ref[:, :half], ratio)
    w, n = eliminate(rest)
    left_ref[:, half:] = close(turned, w, nt)
    right_ref[:, half:] = close(turned, n, nt)
    form = close(left_ref[...], right_ref[...], nt)
    lane = lax.broadcasted_iota(jnp.int32, (block, 2 * block), 1)
    row, column = below(block)
    forms = []
    for k in range(2):
        at = k * 2 * block
        top = form[at : at + block, at : at + 2 * block]
        bottom = form[at + block : at + 2 * block, at : at + 2 * block]
        forms.append(jnp.where(lane < block, top, bottom))
    diagonal = jnp.sum(jnp.where(row == column, forms[1], 0.0), axis=0, keepdims=True)
    packs[core, me] = jnp.where(row <= column, forms[0], forms[1]).astype(BF16)
    pack_ends[core, me] = diagonal

    def both(c, s, peer):
        refs = packs.at[c, s], pack_ends.at[c, s]
        return [send(ref, ref, peer) for ref in refs]

    sent = [both(core, me, (other(o), core)) for o in offsets]

    def unpack(c, s):
        packed = packs[c, s].astype(F32)
        lower = jnp.broadcast_to(pack_ends[c, s], packed.shape)
        for k in range(2):
            spread[c * 2 + k, s] = halved(packed, packed if k == 0 else lower, k).astype(BF16)

    across = [(me, both(core, me, sibling))]
    unpack(core, me)
    arrive = [((z - o[0]) % zs) * 4 + (y + o[1]) % 2 * 2 + (x + o[2]) % 2 for o in offsets]
    for pair, s in reversed(list(zip(sent, arrive))):
        for copy in pair:
            copy.wait()
        across.append((s, both(core, s, sibling)))
        unpack(core, s)
    for s, pair in across:
        for copy in pair:
            copy.wait()
        unpack(1 - core, s)
    load.wait()

    group = 32

    @pl.loop(0, record_ref.shape[0] // group)
    def _(step):
        values = []
        for i in range(group):
            child = step * group + i
            record = record_ref[child]
            parent, place_row = parent_of_ref[0, child], row_block_ref[0, child]
            pushed = dot(spread[place_row // 2, parent], placed(record, place_row % 2))
            values.append(jnp.sum(record.astype(F32) * pushed, axis=0, keepdims=True))
        out_ref[pl.ds(pl.multiple_of(step * group, group), group), :] = (
            jnp.concatenate(values, axis=0) * (2.0 / size)
        )


def strengths(parent_of, row_block, grams, records, parent, eigs, subs, scale):
    children, block, columns = records.shape
    rows, size = parent.shape
    wide, end = (block, 2 * block), (1, 2 * block)
    copies = subs // 2 + 4 * (subs - 1) + 1 + 2 * subs
    vmem = pl.BlockSpec(memory_space=pltpu.VMEM)
    smem = pl.BlockSpec(memory_space=pltpu.SMEM)
    return pl.pallas_call(
        functools.partial(exchange_kernel, subs, scale),
        in_specs=[smem, smem, vmem, pl.BlockSpec(memory_space=pl.ANY), vmem, vmem],
        out_specs=vmem,
        out_shape=jax.ShapeDtypeStruct((children, columns), F32),
        scratch_shapes=[
            pltpu.VMEM(records.shape, BF16),
            pltpu.VMEM((rows // 2, size), F32),
            pltpu.VMEM((size, size), F32),
            pltpu.VMEM((rows // 2, size), F32),
            pltpu.VMEM((rows // 2, size), F32),
            pltpu.VMEM((subs,) + wide, F32),
            pltpu.VMEM((subs,) + end, F32),
            pltpu.VMEM((subs,) + wide, BF16),
            pltpu.VMEM((subs,) + end, F32),
            pltpu.VMEM((subs,) + wide, BF16),
            pltpu.VMEM((subs,) + end, F32),
            pltpu.VMEM((subs,) + wide, BF16),
            pltpu.VMEM((subs,) + end, F32),
            pltpu.VMEM((subs,) + wide, BF16),
            pltpu.VMEM((subs,) + end, F32),
            pltpu.VMEM((2, block + 8, 2 * block), F32),
            pltpu.VMEM((2, subs) + wide, BF16),
            pltpu.VMEM((2, subs) + end, F32),
            pltpu.VMEM((4, subs, block, 2 * block), BF16),
            pltpu.SemaphoreType.DMA,
            pltpu.SemaphoreType.DMA((copies,)),
            pltpu.SemaphoreType.DMA((copies,)),
        ],
        compiler_params=pltpu.CompilerParams(
            collective_id=0, has_side_effects=True, vmem_limit_bytes=32 << 20
        ),
        name="exchange",
    )(parent_of, row_block, grams, records, parent, eigs)


def per_device(
    coupling, coupling_pairs, modes, mode_weights, parent_of, row_block, parent_modes, parent_eigs
):
    subs = lax.axis_size("sub")
    parents = subs * parent_modes.shape[0]
    children = coupling.shape[0]
    parent_of, row_block = parent_of.reshape(1, children), row_block.reshape(1, children)
    records, grams = records_and_grams(
        parent_of, row_block, coupling_pairs.T, coupling, modes, mode_weights, parents
    )
    scale = 1.0 / (children * modes.shape[2] * lax.axis_size("mode"))
    return strengths(
        parent_of, row_block, grams, records, parent_modes[0], parent_eigs, subs, scale
    )


def solution(mesh):
    in_specs = (
        P("sub", None, None),
        P("sub", None),
        P("sub", None, "mode"),
        P("sub", "mode"),
        P("sub", None),
        P("sub"),
        P("sub", None, None),
        P("sub", None),
    )
    return jax.shard_map(
        per_device, mesh=mesh, in_specs=in_specs, out_specs=P("sub", "mode"), check_vma=False
    )
```
